32 devices in a mesh: dp: 8 (over z, x), tensor: 4 (over y, core).
Axes of the slice: x: 2, y: 2, z: 4, core: 2. Of those that a mesh axis runs over, the one named last changes fastest.
Arguments:
- inputs: bfloat16 [8, 1024, 2048], P('dp'), may hold values from -6 to 6
- lengths: int32 [8], P('dp'), may hold values from 256 to 1024, as said below
- loss_mask: int32 [8, 1024], P('dp'), may hold values 0 or 1
- teacher: bfloat16 [8, 1024, 2048], P('dp'), may hold values from -6 to 6
- attn_gain: bfloat16 [2048], P('dp'), may hold values from 0.5 to 1.5
- q_weight: bfloat16 [2048, 2048], P('dp', 'tensor'), may hold values from -0.125 to 0.125
- k_weight: bfloat16 [2048, 2048], P('dp', 'tensor'), may hold values from -0.125 to 0.125
- v_weight: bfloat16 [2048, 4096], P('dp', 'tensor'), may hold values from -0.125 to 0.125
- gating_weight: bfloat16 [2048, 4096], P('dp', 'tensor'), may hold values from -0.125 to 0.125
- alpha_weight: bfloat16 [2048, 16], P('dp', 'tensor'), may hold values from -0.125 to 0.125
- beta_weight: bfloat16 [2048, 16], P('dp', 'tensor'), may hold values from -0.125 to 0.125
- q_conv: float32 [4, 2048], P(None, 'tensor'), may hold values from -3 to 3
- k_conv: float32 [4, 2048], P(None, 'tensor'), may hold values from -3 to 3
- v_conv: float32 [4, 4096], P(None, 'tensor'), may hold values from -3 to 3
- decay_log: float32 [16], P('tensor'), may hold values from -1 to 0.5
- decay_bias: float32 [16], P('tensor'), may hold values from -6 to -1
- out_gain: float32 [256], replicated, may hold values from 0.5 to 1.5
- out_weight: bfloat16 [4096, 2048], P('tensor', 'dp'), may hold values from -0.1875 to 0.1875
- ffn_gain: bfloat16 [2048], P('dp'), may hold values from 0.5 to 1.5
- ffn_gate: bfloat16 [2048, 5632], P('dp', 'tensor'), may hold values from -0.125 to 0.125
- ffn_up: bfloat16 [2048, 5632], P('dp', 'tensor'), may hold values from -0.125 to 0.125
- ffn_down: bfloat16 [5632, 2048], P('tensor', 'dp'), may hold values from -0.15625 to 0.15625
Outputs:
- activations: bfloat16 [8, 1024, 2048], P('dp', 'tensor')
- loss: float32 [], replicated
- input_grad: float32 [8, 1024, 2048], P('dp', 'tensor')
- attn_gain_grad: float32 [2048], P('dp')
- q_weight_grad: float32 [2048, 2048], P('dp', 'tensor')
- k_weight_grad: float32 [2048, 2048], P('dp', 'tensor')
- v_weight_grad: float32 [2048, 4096], P('dp', 'tensor')
- gating_weight_grad: float32 [2048, 4096], P('dp', 'tensor')
- alpha_weight_grad: float32 [2048, 16], P('dp', 'tensor')
- beta_weight_grad: float32 [2048, 16], P('dp', 'tensor')
- q_conv_grad: float32 [4, 2048], P(None, 'tensor')
- k_conv_grad: float32 [4, 2048], P(None, 'tensor')
- v_conv_grad: float32 [4, 4096], P(None, 'tensor')
- decay_log_grad: float32 [16], P('tensor')
- decay_bias_grad: float32 [16], P('tensor')
- out_gain_grad: float32 [256], replicated
- out_weight_grad: float32 [4096, 2048], P('tensor', 'dp')
- ffn_gain_grad: float32 [2048], P('dp')
- ffn_gate_grad: float32 [2048, 5632], P('dp', 'tensor')
- ffn_up_grad: float32 [2048, 5632], P('dp', 'tensor')
- ffn_down_grad: float32 [5632, 2048], P('tensor', 'dp')
The draws below stay inside these ranges and needn't reach their ends.
Inputs may be any that keep to these rules, and one draw needn't show every extreme that they name: A sequence's valid tokens are its first lengths slots; in every draw one sequence has 1024 and another 256.
All inputs are finite; a program needn't handle non-finite values. No bound on the sum of `loss_mask` on one device may be relied on, other than what follows from the above.
Results may differ from the reference program's by a relative error of at most 0.018.
Values may be sent and summed in bfloat16 or wider, within the bound.
A program may use at most 320 MiB of HBM per device.

```python
import jax
import jax.numpy as jnp
from jax import lax

D = 2048
HEADS = 16
DV = 256
FF = 5632
KW = 4
SPAN = 64
SLOTS = 1024
LEN_MIN = 256
SEQS = 8
TOKENS = 8192
HK = 2048
HV = 4096


def draw_lengths(key, part):
    keys_all = jax.random.split(jax.random.fold_in(key, 17), 3)
    drawn = jax.random.randint(keys_all[0], (SEQS,), LEN_MIN, SLOTS + 1)
    longest = jax.random.randint(keys_all[1], (), 0, SEQS)
    shortest = (longest + 1 + jax.random.randint(keys_all[2], (), 0, SEQS - 1)) % SEQS
    seq_index = jnp.arange(SEQS, dtype=jnp.int32)
    drawn = jnp.where(seq_index == longest, SLOTS, drawn)
    drawn = jnp.where(seq_index == shortest, LEN_MIN, drawn)
    return drawn.astype(jnp.int32)


def plant(values, key, smallest, high):
    dims = values.shape
    place = [jax.random.randint(jax.random.fold_in(key, axis), (), 0, dims[axis]) for axis in range(len(dims))]
    values = values.at[tuple(place)].set(smallest)
    longest = dims.index(max(dims))
    place[longest] = (place[longest] + 1) % dims[longest]
    return values.at[tuple(place)].set(high)


def level_of(key, extent, cuts, least, largest):
    def one(dim, shards_of):
        heights = jax.random.uniform(jax.random.fold_in(jax.random.fold_in(key, 6), dim), (shards_of,), jnp.float32, least / len(cuts), largest / len(cuts))
        return jnp.repeat(jnp.exp(heights), extent[dim] // shards_of).reshape((-1,) + (1,) * (len(extent) - dim - 1))

    level = one(*cuts[0])
    for cut in cuts[1:]:
        level = level * one(*cut)
    return level


def normal_values(stream_key, shape, scale, bound, cuts=(), kind=jnp.bfloat16):
    values = scale * jax.random.normal(stream_key, shape, jnp.float32)
    if cuts:
        values = values * level_of(stream_key, shape, cuts, -0.22, 0.18)
    return jnp.clip(values, -bound, bound).astype(kind)


def setup_inputs(seed: int = 0) -> dict:
    arg_keys = jax.random.split(jax.random.key(seed), 23)
    inputs = normal_values(arg_keys[0], (SEQS, SLOTS, D), 1.0, 6.0, ((0, 8),))
    lengths = draw_lengths(jax.random.fold_in(arg_keys[22], 71), 0)
    loss_mask = plant((jax.random.randint(arg_keys[2], (SEQS, SLOTS), 0, 4) < 3).astype(jnp.int32), jax.random.fold_in(arg_keys[2], 1), 0, 1)
    teacher = normal_values(arg_keys[3], (SEQS, SLOTS, D), 1.0, 6.0, ((0, 8),))
    attn_gain = jnp.clip(1.0 + 0.1 * jax.random.normal(arg_keys[4], (D,), jnp.float32), 0.5, 1.5).astype(jnp.bfloat16)
    q_weight = normal_values(arg_keys[5], (D, HK), D ** -0.5, 0.125, ((0, 8), (1, 4)))
    k_weight = normal_values(arg_keys[6], (D, HK), D ** -0.5, 0.125, ((0, 8), (1, 4)))
    v_weight = normal_values(arg_keys[7], (D, HV), D ** -0.5, 0.125, ((0, 8), (1, 4)))
    gating_weight = normal_values(arg_keys[8], (D, HV), D ** -0.5, 0.125, ((0, 8), (1, 4)))
    alpha_weight = normal_values(arg_keys[9], (D, HEADS), D ** -0.5, 0.125, ((0, 8), (1, 4)))
    beta_weight = normal_values(arg_keys[10], (D, HEADS), D ** -0.5, 0.125, ((0, 8), (1, 4)))
    q_conv = normal_values(arg_keys[11], (KW, HK), 0.5, 3.0, ((1, 4),), jnp.float32)
    k_conv = normal_values(arg_keys[12], (KW, HK), 0.5, 3.0, ((1, 4),), jnp.float32)
    v_conv = normal_values(arg_keys[13], (KW, HV), 0.5, 3.0, ((1, 4),), jnp.float32)
    decay_log = jnp.clip(-1.0 + 1.5 * jax.random.uniform(arg_keys[14], (HEADS,), jnp.float32) ** level_of(arg_keys[14], (HEADS,), ((0, 4),), -0.2, 0.2), -1.0, 0.5)
    decay_bias = jnp.clip(-6.0 + 5.0 * jax.random.uniform(arg_keys[15], (HEADS,), jnp.float32) ** level_of(arg_keys[15], (HEADS,), ((0, 4),), -0.2, 0.2), -6.0, -1.0)
    out_gain = jnp.clip(1.0 + 0.1 * jax.random.normal(arg_keys[16], (DV,), jnp.float32), 0.5, 1.5)
    out_weight = normal_values(arg_keys[17], (HV, D), (HV // 4) ** -0.5, 0.1875, ((0, 4), (1, 8)))
    ffn_gain = jnp.clip(1.0 + 0.1 * jax.random.normal(arg_keys[18], (D,), jnp.float32), 0.5, 1.5).astype(jnp.bfloat16)
    ffn_gate = normal_values(arg_keys[19], (D, FF), D ** -0.5, 0.125, ((0, 8), (1, 4)))
    ffn_up = normal_values(arg_keys[20], (D, FF), D ** -0.5, 0.125, ((0, 8), (1, 4)))
    ffn_down = normal_values(arg_keys[21], (FF, D), (FF // 4) ** -0.5, 0.15625, ((0, 4), (1, 8)))
    return {"inputs": inputs, "lengths": lengths, "loss_mask": loss_mask, "teacher": teacher, "attn_gain": attn_gain, "q_weight": q_weight, "k_weight": k_weight, "v_weight": v_weight, "gating_weight": gating_weight, "alpha_weight": alpha_weight, "beta_weight": beta_weight, "q_conv": q_conv, "k_conv": k_conv, "v_conv": v_conv, "decay_log": decay_log, "decay_bias": decay_bias, "out_gain": out_gain, "out_weight": out_weight, "ffn_gain": ffn_gain, "ffn_gate": ffn_gate, "ffn_up": ffn_up, "ffn_down": ffn_down}


@jax.custom_vjp
def low(v):
    return lax.optimization_barrier(v.astype(jnp.bfloat16)).astype(jnp.float32)

@jax.custom_vjp
def low_back(v):
    return v

def low_keep(v):
    return (low(v), None)

def low_pass(kept, grad):
    return (grad,)

def back_keep(v):
    return (v, None)

def back_low(kept, grad):
    return (low(grad),)
low.defvjp(low_keep, low_pass)
low_back.defvjp(back_keep, back_low)

def causal_conv(values, kernel):
    kernel_len = kernel.shape[0]
    length = values.shape[1]
    padded = jnp.pad(values, ((0, 0), (kernel_len - 1, 0), (0, 0)))
    summed = padded[:, 0:length, :] * kernel[0]
    for offset in range(1, kernel_len):
        summed = summed + padded[:, offset:offset + length, :] * kernel[offset]
    return jax.nn.silu(summed)

def unit_rows(values):
    return values * lax.rsqrt(lax.optimization_barrier(jnp.sum(values * values, -1, keepdims=True)) + 1e-06)

def to_blocks(values, block_len):
    batch_n = values.shape[0]
    count_n = values.shape[1] // block_len
    shaped = values.reshape((batch_n, count_n, block_len) + values.shape[2:])
    if values.ndim == 4:
        return shaped.transpose(1, 0, 3, 2, 4)
    return shaped.transpose(1, 0, 3, 2)

def delta_block(memory, block):
    queries, key_rows, values, beta_val, decays = block
    block_len = decays.shape[-1]
    highest = lax.Precision.HIGHEST
    cumulative = jnp.cumsum(decays, -1)
    spread = cumulative[..., :, None] - cumulative[..., None, :]
    row_index = lax.broadcasted_iota(jnp.int32, (block_len, block_len), 0)
    col_index = lax.broadcasted_iota(jnp.int32, (block_len, block_len), 1)
    strict = row_index > col_index
    within = row_index >= col_index
    key_decay = jnp.exp(jnp.where(strict, spread, 0.0)) * strict.astype(jnp.float32)
    key_mix = jnp.einsum('bhid,bhjd->bhij', key_rows * beta_val[..., None], key_rows, precision=highest) * key_decay
    identity = jnp.eye(block_len, dtype=decays.dtype)
    right_side = jnp.concatenate([key_rows * (beta_val * jnp.exp(cumulative))[..., None], values * beta_val[..., None]], -1)
    solved = jax.scipy.linalg.solve_triangular(identity + key_mix, right_side, lower=True, unit_diagonal=True)
    key_dim = key_rows.shape[-1]
    fresh_vals = solved[..., key_dim:] - jnp.einsum('bhcd,bhde->bhce', solved[..., :key_dim], memory, precision=highest)
    query_decay = jnp.exp(jnp.where(within, spread, 0.0)) * within.astype(jnp.float32)
    scores = jnp.einsum('bhid,bhjd->bhij', queries, key_rows, precision=highest) * query_decay
    result = jnp.einsum('bhcd,bhde->bhce', queries * jnp.exp(cumulative)[..., None], memory, precision=highest)
    result = result + jnp.einsum('bhij,bhje->bhie', scores, fresh_vals, precision=highest)
    final_sum = cumulative[..., -1]
    carried = jnp.exp(final_sum)[..., None, None] * memory + jnp.einsum('bhcd,bhce->bhde', key_rows * jnp.exp(final_sum[..., None] - cumulative)[..., None], fresh_vals, precision=highest)
    return (carried, result)

def mixer(q_proj, k_proj, v_proj, g_proj, a_proj, b_proj, q_kernel, k_kernel, v_kernel, decay_log, decay_bias, out_gain):
    batch_n, length, head_n = a_proj.shape
    queries = unit_rows(causal_conv(q_proj, q_kernel).reshape(batch_n, length, head_n, -1))
    queries = queries * queries.shape[-1] ** (-0.5)
    key_rows = unit_rows(causal_conv(k_proj, k_kernel).reshape(batch_n, length, head_n, -1))
    values = causal_conv(v_proj, v_kernel).reshape(batch_n, length, head_n, -1)
    beta_val = jax.nn.sigmoid(b_proj)
    decays = -jnp.exp(decay_log) * jax.nn.softplus(a_proj + decay_bias)
    memory = jnp.zeros((batch_n, head_n, key_rows.shape[-1], values.shape[-1]), q_proj.dtype)
    blocks = (to_blocks(queries, SPAN), to_blocks(key_rows, SPAN), to_blocks(values, SPAN), to_blocks(beta_val, SPAN), to_blocks(decays, SPAN))
    memory, outputs = lax.scan(jax.checkpoint(delta_block), memory, blocks)
    merged = outputs.transpose(1, 0, 3, 2, 4).reshape(batch_n, length, head_n, -1)
    gating = g_proj.reshape(batch_n, length, head_n, -1)
    normed = merged * lax.rsqrt(lax.optimization_barrier(jnp.mean(merged * merged, -1, keepdims=True)) + 1e-05) * out_gain * jax.nn.silu(gating)
    return normed.reshape(batch_n, length, -1)

def norm_rows(values, gain):
    return values * lax.rsqrt(lax.optimization_barrier(jnp.mean(values * values, -1, keepdims=True)) + 1e-06) * gain

def forward(params, inputs, teacher, tok_weight):
    attn_gain, q_weight, k_weight, v_weight, gating_weight, alpha_weight, beta_weight, q_conv, k_conv, v_conv, decay_log, decay_bias, out_gain, out_weight, ffn_gain, ffn_gate, ffn_up, ffn_down = params
    highest = lax.Precision.HIGHEST

    def project(source, weight):
        return low_back(jnp.einsum('bsd,de->bse', source, weight, precision=highest))
    normed = low(norm_rows(inputs, attn_gain))
    mixed = low(mixer(project(normed, q_weight), project(normed, k_weight), project(normed, v_weight), project(normed, gating_weight), project(normed, alpha_weight), project(normed, beta_weight), q_conv, k_conv, v_conv, decay_log, decay_bias, out_gain))
    attention = low_back(jnp.einsum('bse,ed->bsd', mixed, out_weight, precision=highest))
    resid = inputs + attention
    normed_ffn = low(norm_rows(resid, ffn_gain))
    gate_pre = project(normed_ffn, ffn_gate)
    up_pre = project(normed_ffn, ffn_up)
    hidden = low(jax.nn.silu(gate_pre) * up_pre)
    output = resid + low_back(jnp.einsum('bsf,fd->bsd', hidden, ffn_down, precision=highest))
    error = (output - teacher) * tok_weight[..., None]
    return (jnp.sum(error * error), output)

def reference(inputs, lengths, loss_mask, teacher, attn_gain, q_weight, k_weight, v_weight, gating_weight, alpha_weight, beta_weight, q_conv, k_conv, v_conv, decay_log, decay_bias, out_gain, out_weight, ffn_gain, ffn_gate, ffn_up, ffn_down):
    params = tuple((weight_arg.astype(jnp.float32) for weight_arg in (attn_gain, q_weight, k_weight, v_weight, gating_weight, alpha_weight, beta_weight, q_conv, k_conv, v_conv, decay_log, decay_bias, out_gain, out_weight, ffn_gain, ffn_gate, ffn_up, ffn_down)))
    positions = jnp.arange(SLOTS, dtype=jnp.int32)
    valid = (positions[None, :] < lengths[:, None]).astype(jnp.float32)
    tok_weight = valid * loss_mask.astype(jnp.float32)
    token_count = jnp.sum(tok_weight)
    coef = 0.5 * TOKENS / token_count
    seq_total = inputs.shape[0]
    group_n = 4 if seq_total % 4 == 0 else 1

    def grouped(array):
        return array.reshape((seq_total // group_n, group_n) + array.shape[1:])
    stacked = (grouped(inputs.astype(jnp.float32)), grouped(teacher.astype(jnp.float32)), grouped(tok_weight))

    def step_fn(carry, batch):
        grad_sum, error_total = carry
        group_in, group_teacher, group_weight = batch

        def loss_fn(params_in, input_in):
            return forward(params_in, input_in, group_teacher, group_weight)
        squared, back_fn, output = jax.vjp(loss_fn, params, group_in, has_aux=True)
        param_grads, input_grad = back_fn(coef)
        grad_sum = jax.tree.map(jnp.add, grad_sum, param_grads)
        return ((grad_sum, error_total + squared), (output, input_grad))
    zero_grads = jax.tree.map(jnp.zeros_like, params)
    (grad_sum, error_total), (outputs, input_grads) = lax.scan(step_fn, (zero_grads, jnp.zeros((), jnp.float32)), stacked)
    activations = (outputs.reshape(inputs.shape) * valid[..., None]).astype(jnp.bfloat16)
    loss = error_total / token_count
    return (activations, loss, input_grads.reshape(inputs.shape), grad_sum[0], grad_sum[1], grad_sum[2], grad_sum[3], grad_sum[4], grad_sum[5], grad_sum[6], grad_sum[7], grad_sum[8], grad_sum[9], grad_sum[10], grad_sum[11], grad_sum[12], grad_sum[13], grad_sum[14], grad_sum[15], grad_sum[16], grad_sum[17])
```

```python
import functools
import jax
import jax.numpy as jnp
from jax import lax
from jax.experimental import pallas as pl
from jax.experimental.pallas import tpu as pltpu
from jax.sharding import PartitionSpec as P

BLOCK = 128
BF = jnp.bfloat16
F32 = jnp.float32


def mm(a, b, dims=((1,), (0,))):
    return lax.dot_general(a.astype(BF), b.astype(BF), (dims, ((), ())), preferred_element_type=F32)


def mm_nt(a, b):
    return mm(a, b, ((1,), (1,)))


def mm_tn(a, b):
    return mm(a, b, ((0,), (0,)))


def split(a):
    high = a.astype(BF)
    return high, (a - high.astype(F32)).astype(BF)


def mm3(a, b):
    ah, al = a
    bh, bl = b
    return mm(ah, bh) + (mm(ah, bl) + mm(al, bh))


def exact(a, b):
    return lax.dot_general(a, b, (((1,), (0,)), ((), ())), precision=lax.Precision.HIGHEST, preferred_element_type=F32)


def indices():
    rows = lax.broadcasted_iota(jnp.int32, (BLOCK, BLOCK), 0)
    cols = lax.broadcasted_iota(jnp.int32, (BLOCK, BLOCK), 1)
    return rows, cols


def unit_lower_inverse(strict, rows, cols):
    near = jnp.where((rows // 8) == (cols // 8), strict, 0.0)
    eye = (rows == cols).astype(F32)
    first = split(-near)
    second = mm3(first, first)
    second_s = split(second)
    fourth_s = split(mm3(second_s, second_s))
    total = eye - near
    total = total + mm3(split(total), second_s)
    total = total + mm3(split(total), fourth_s)
    size = 8
    while size < BLOCK:
        pick = ((rows // size) == (cols // size) + 1) & ((rows // size) % 2 == 1)
        lower = split(jnp.where(pick, strict, 0.0))
        total_s = split(total)
        total = total - mm3(total_s, split(mm3(lower, total_s)))
        size *= 2
    return total


def decay_terms(ab, hp, rows, cols):
    shifted = ab + hp[1:2, :]
    soft = jnp.maximum(shifted, 0.0) + jnp.log1p(jnp.exp(-jnp.abs(shifted)))
    decay = hp[0:1, :] * soft
    lower = (rows >= cols).astype(F32)
    cum = exact(lower, decay)
    return shifted, decay, cum


def conv_silu(ext_ref, taps, start, width):
    cols = slice(start, start + width)
    total = ext_ref[5 : 5 + BLOCK, cols] * taps[0:1, cols]
    for tap in range(1, 4):
        total = total + ext_ref[5 + tap : 5 + tap + BLOCK, cols] * taps[tap : tap + 1, cols]
    sig = jax.nn.sigmoid(total)
    return total, sig


def forward_kernel(
    heads, dk, dv, proj_ref, taps_ref, hp_ref, gain_ref,
    mixed_ref, o_ref, f_ref, t_ref, s_ref, state, ext,
):
    hk, hv = heads * dk, heads * dv
    wide = 2 * hk + hv

    @pl.when(pl.program_id(0) == 0)
    def _():
        state[...] = jnp.zeros_like(state)
        ext[0:8, :] = jnp.zeros((8, wide), F32)

    @pl.when(pl.program_id(0) > 0)
    def _():
        ext[0:8, :] = ext[BLOCK : BLOCK + 8, :]

    ext[8 : 8 + BLOCK, :] = proj_ref[:, 0:wide].astype(F32)
    rows, cols = indices()
    ab = proj_ref[:, wide + hv :].astype(F32)
    _, _, cum = decay_terms(ab, hp_ref[...], rows, cols)
    beta_all = jax.nn.sigmoid(ab)
    cum_t = cum.T
    within = rows >= cols
    strict = rows > cols
    taps = taps_ref[...]
    gain = gain_ref[...]
    s_ref[0] = state[...].astype(s_ref.dtype)
    for h in range(heads):
        raw, sig = conv_silu(ext, taps, h * dk, dk)
        act = raw * sig
        query = act * (lax.rsqrt(jnp.sum(act * act, -1, keepdims=True) + 1e-06) * dk ** (-0.5))
        raw, sig = conv_silu(ext, taps, hk + h * dk, dk)
        act = raw * sig
        key = act * lax.rsqrt(jnp.sum(act * act, -1, keepdims=True) + 1e-06)
        raw, sig = conv_silu(ext, taps, 2 * hk + h * dv, dv)
        value = raw * sig
        beta = beta_all[:, heads + h : heads + h + 1]
        c_col = cum[:, h : h + 1]
        c_row = cum_t[h : h + 1, :]
        c_last = cum[BLOCK - 1 : BLOCK, h : h + 1]
        fade = jnp.exp(jnp.where(within, c_col - c_row, 0.0))
        key_b = key.astype(BF)
        query_b = query.astype(BF)
        mix = jnp.where(strict, mm_nt(key_b, key_b) * fade * beta, 0.0)
        inverse = unit_lower_inverse(mix, rows, cols)
        inv_b = inverse.astype(BF)
        t_ref[:, h * BLOCK : (h + 1) * BLOCK] = inv_b
        grow = jnp.exp(c_col)
        w_rows = mm(inv_b, key * (beta * grow))
        u_rows = mm(inv_b, value * beta)
        memory = state[h * dk : (h + 1) * dk, :]
        mem_b = memory.astype(BF)
        fresh = u_rows - mm(w_rows, mem_b)
        fresh_b = fresh.astype(BF)
        f_ref[:, h * dv : (h + 1) * dv] = fresh_b
        scores = jnp.where(within, mm_nt(query_b, key_b) * fade, 0.0)
        out = mm(query_b, mem_b) * grow + mm(scores, fresh_b)
        state[h * dk : (h + 1) * dk, :] = jnp.exp(c_last) * memory + mm_tn(
            key * jnp.exp(c_last - c_col), fresh_b
        )
        o_ref[:, h * dv : (h + 1) * dv] = out.astype(o_ref.dtype)
        gate = proj_ref[:, wide + h * dv : wide + (h + 1) * dv].astype(F32)
        scale = lax.rsqrt(jnp.mean(out * out, -1, keepdims=True) + 1e-05)
        mixed_ref[:, h * dv : (h + 1) * dv] = (
            out * scale * gain * (gate * jax.nn.sigmoid(gate))
        ).astype(mixed_ref.dtype)


def delta_forward(proj, taps, hp, gain, heads, dk, dv, store=BF):
    rows = proj.shape[0]
    steps = rows // BLOCK
    wide = 2 * heads * dk + heads * dv
    width = proj.shape[1]
    hv = heads * dv

    def by_step(cols):
        return pl.BlockSpec((BLOCK, cols), lambda i: (i, 0))

    def fixed(shape):
        return pl.BlockSpec(shape, lambda i: (0, 0))

    return pl.pallas_call(
        functools.partial(forward_kernel, heads, dk, dv),
        grid=(steps,),
        in_specs=[by_step(width), fixed(taps.shape), fixed(hp.shape), fixed(gain.shape)],
        out_specs=[
            by_step(hv), by_step(hv), by_step(hv), by_step(heads * BLOCK),
            pl.BlockSpec((1, heads * dk, dv), lambda i: (i, 0, 0)),
        ],
        out_shape=[
            jax.ShapeDtypeStruct((rows, hv), BF),
            jax.ShapeDtypeStruct((rows, hv), store),
            jax.ShapeDtypeStruct((rows, hv), BF),
            jax.ShapeDtypeStruct((rows, heads * BLOCK), BF),
            jax.ShapeDtypeStruct((steps, heads * dk, dv), BF),
        ],
        scratch_shapes=[
            pltpu.VMEM((heads * dk, dv), F32),
            pltpu.VMEM((BLOCK + 8, wide), F32),
        ],
        compiler_params=pltpu.CompilerParams(dimension_semantics=("arbitrary",)),
        cost_estimate=pl.CostEstimate(flops=6 * rows * heads * 128 * 128 * 10, bytes_accessed=rows * 30000, transcendentals=0),
    )(proj, taps, hp, gain)


def unit_back(act, scale, grad):
    return scale * grad - act * (scale * scale * scale) * jnp.sum(grad * act, -1, keepdims=True)


def silu_back(raw, sig, grad):
    return grad * (sig * (1.0 + raw * (1.0 - sig)))


def backward_kernel(
    heads, dk, dv, proj_ref, halo_ref, taps_ref, hp_ref, gain_ref, o_ref, f_ref, t_ref, s_ref, dm_ref,
    dproj_ref, dtaps_ref, dhp_ref, dgain_ref, dstate, ext, dext,
):
    hk, hv = heads * dk, heads * dv
    wide = 2 * hk + hv
    step = pl.program_id(0)
    last = pl.num_programs(0) - 1

    @pl.when(step == 0)
    def _():
        dstate[...] = jnp.zeros_like(dstate)
        dext[BLOCK : BLOCK + 8, :] = jnp.zeros((8, wide), F32)
        dtaps_ref[...] = jnp.zeros_like(dtaps_ref)
        dhp_ref[...] = jnp.zeros_like(dhp_ref)
        dgain_ref[...] = jnp.zeros_like(dgain_ref)

    @pl.when(step > 0)
    def _():
        dext[BLOCK : BLOCK + 8, :] = dext[0:8, :]

    ext[0:8, :] = jnp.where(step == last, 0.0, halo_ref[:, 0:wide].astype(F32))
    ext[8 : 8 + BLOCK, :] = proj_ref[:, 0:wide].astype(F32)
    rows, cols = indices()
    ab = proj_ref[:, wide + hv :].astype(F32)
    hp = hp_ref[...]
    shifted, decay, cum = decay_terms(ab, hp, rows, cols)
    beta_all = jax.nn.sigmoid(ab)
    cum_t = cum.T
    within = rows >= cols
    strict = rows > cols
    taps = taps_ref[...]
    gain = gain_ref[...]
    lane = cols
    dbeta_all = jnp.zeros((BLOCK, BLOCK), F32)
    dcum_all = jnp.zeros((BLOCK, BLOCK), F32)
    dcum_rows = jnp.zeros((BLOCK, BLOCK), F32)
    dlast_all = jnp.zeros((1, BLOCK), F32)
    dgain = jnp.zeros((1, dv), F32)
    for h in range(heads):
        q_cols = slice(h * dk, (h + 1) * dk)
        k_cols = slice(hk + h * dk, hk + (h + 1) * dk)
        v_cols = slice(2 * hk + h * dv, 2 * hk + (h + 1) * dv)
        o_cols = slice(h * dv, (h + 1) * dv)
        gate = proj_ref[:, wide + h * dv : wide + (h + 1) * dv].astype(F32)
        out = o_ref[:, o_cols].astype(F32)
        d_mixed = dm_ref[:, o_cols].astype(F32)
        scale = lax.rsqrt(jnp.mean(out * out, -1, keepdims=True) + 1e-05)
        sig = jax.nn.sigmoid(gate)
        base = out * scale * d_mixed
        dgain = dgain + jnp.sum(base * (gate * sig), 0, keepdims=True)
        dproj_ref[:, wide + h * dv : wide + (h + 1) * dv] = silu_back(gate, sig, base * gain).astype(dproj_ref.dtype)
        d_normed = d_mixed * gain * (gate * sig)
        d_out = scale * d_normed - out * (scale * scale * scale) * jnp.mean(d_normed * out, -1, keepdims=True)
        d_out_b = d_out.astype(BF)
        q_raw, q_sig = conv_silu(ext, taps, h * dk, dk)
        q_act = q_raw * q_sig
        q_scale = lax.rsqrt(jnp.sum(q_act * q_act, -1, keepdims=True) + 1e-06)
        query = q_act * (q_scale * dk ** (-0.5))
        k_raw, k_sig = conv_silu(ext, taps, hk + h * dk, dk)
        k_act = k_raw * k_sig
        k_scale = lax.rsqrt(jnp.sum(k_act * k_act, -1, keepdims=True) + 1e-06)
        key = k_act * k_scale
        v_raw, v_sig = conv_silu(ext, taps, 2 * hk + h * dv, dv)
        value = v_raw * v_sig
        beta = beta_all[:, heads + h : heads + h + 1]
        c_col = cum[:, h : h + 1]
        c_row = cum_t[h : h + 1, :]
        c_last = cum[BLOCK - 1 : BLOCK, h : h + 1]
        fade = jnp.exp(jnp.where(within, c_col - c_row, 0.0))
        key_b = key.astype(BF)
        query_b = query.astype(BF)
        grow = jnp.exp(c_col)
        rest = jnp.exp(c_last - c_col)
        kk = jnp.where(strict, mm_nt(key_b, key_b) * fade, 0.0)
        scores = jnp.where(within, mm_nt(query_b, key_b) * fade, 0.0)
        inv_b = t_ref[:, h * BLOCK : (h + 1) * BLOCK]
        fresh_b = f_ref[:, o_cols]
        mem_b = s_ref[0, h * dk : (h + 1) * dk, :]
        d_mem = dstate[h * dk : (h + 1) * dk, :]
        d_mem_b = d_mem.astype(BF)
        d_fresh = mm_tn(scores, d_out_b) + mm(key * rest, d_mem_b)
        d_right = mm_tn(inv_b, d_fresh)
        d_right_b = d_right.astype(BF)
        d_scores = jnp.where(within, mm_nt(d_out_b, fresh_b), 0.0)
        d_mix = jnp.where(strict, -mm_nt(d_right_b, fresh_b), 0.0)
        x_rows = mm_nt(d_right_b, mem_b)
        y_rows = mm_nt(d_out_b, mem_b)
        z_rows = mm_nt(fresh_b, d_mem_b)
        decay_all = jnp.exp(c_last)
        dstate[h * dk : (h + 1) * dk, :] = (
            decay_all * d_mem
            + mm_tn(query * grow, d_out_b)
            - mm_tn(key * (beta * grow), d_right_b)
        )
        x_sum = jnp.sum(x_rows * key, -1, keepdims=True)
        y_sum = jnp.sum(y_rows * query, -1, keepdims=True)
        z_sum = jnp.sum(z_rows * key, -1, keepdims=True) * rest
        mix_part = d_mix * kk
        d_beta = (
            jnp.sum(d_right * value, -1, keepdims=True)
            - grow * x_sum
            + jnp.sum(mix_part, -1, keepdims=True)
        )
        pair = d_scores * scores + mix_part * beta
        d_cum = jnp.sum(pair, -1, keepdims=True) + grow * (y_sum - beta * x_sum) - z_sum
        d_last = jnp.sum(z_sum, 0, keepdims=True) + decay_all * jnp.sum(
            jnp.sum(d_mem * mem_b.astype(F32), -1, keepdims=True), 0, keepdims=True
        )
        dbeta_all = jnp.where(lane == heads + h, d_beta, dbeta_all)
        dcum_all = jnp.where(lane == h, d_cum, dcum_all)
        dcum_rows = jnp.where(rows == h, jnp.sum(pair, 0, keepdims=True), dcum_rows)
        dlast_all = jnp.where(lane[0:1, :] == h, d_last, dlast_all)
        g_scores = (d_scores * fade).astype(BF)
        g_mix = (d_mix * fade * beta).astype(BF)
        d_query = grow * y_rows + mm(g_scores, key_b)
        d_key = (
            rest * z_rows - (beta * grow) * x_rows
            + mm_tn(g_scores, query_b) + mm(g_mix, key_b) + mm_tn(g_mix, key_b)
        )
        d_value = d_right * beta
        dext[0:BLOCK, q_cols] = silu_back(q_raw, q_sig, unit_back(q_act, q_scale, d_query * dk ** (-0.5)))
        dext[0:BLOCK, k_cols] = silu_back(k_raw, k_sig, unit_back(k_act, k_scale, d_key))
        dext[0:BLOCK, v_cols] = silu_back(v_raw, v_sig, d_value)
    dgain_ref[...] += dgain
    d_cum = dcum_all - dcum_rows.T + jnp.where(rows == BLOCK - 1, dlast_all, 0.0)
    upper = (rows <= cols).astype(F32)
    d_decay = exact(upper, d_cum)
    d_alpha = d_decay * hp[0:1, :] * jax.nn.sigmoid(shifted)
    d_ab = d_alpha + dbeta_all * beta_all * (1.0 - beta_all)
    dproj_ref[:, wide + hv :] = d_ab.astype(dproj_ref.dtype)
    dhp_ref[0:1, :] += jnp.sum(d_decay * decay, 0, keepdims=True)
    dhp_ref[1:2, :] += jnp.sum(d_alpha, 0, keepdims=True)
    chunk = 256
    for start in range(0, wide, chunk):
        part = slice(start, start + chunk)
        d_conv = dext[0:BLOCK, part]
        total = dext[3 : 3 + BLOCK, part] * taps[0:1, part]
        dtaps_ref[0:1, part] += jnp.sum(d_conv * ext[5 : 5 + BLOCK, part], 0, keepdims=True)
        for tap in range(1, 4):
            total = total + dext[3 - tap : 3 - tap + BLOCK, part] * taps[tap : tap + 1, part]
            dtaps_ref[tap : tap + 1, part] += jnp.sum(d_conv * ext[5 + tap : 5 + tap + BLOCK, part], 0, keepdims=True)
        dproj_ref[:, part] = total.astype(dproj_ref.dtype)


def delta_backward(proj, taps, hp, gain, out, fresh, inverse, states, d_mixed, heads, dk, dv):
    rows, width = proj.shape
    steps = rows // BLOCK
    wide = 2 * heads * dk + heads * dv
    hv = heads * dv

    def by_step(cols):
        return pl.BlockSpec((BLOCK, cols), lambda i: (steps - 1 - i, 0))

    def fixed(shape):
        return pl.BlockSpec(shape, lambda i: (0, 0))

    per = BLOCK // 8
    return pl.pallas_call(
        functools.partial(backward_kernel, heads, dk, dv),
        grid=(steps,),
        in_specs=[
            by_step(width),
            pl.BlockSpec((8, width), lambda i: (jnp.maximum((steps - 1 - i) * per - 1, 0), 0)),
            fixed(taps.shape), fixed(hp.shape), fixed(gain.shape),
            by_step(hv), by_step(hv), by_step(heads * BLOCK),
            pl.BlockSpec((1, heads * dk, dv), lambda i: (steps - 1 - i, 0, 0)),
            by_step(hv),
        ],
        out_specs=[by_step(width), fixed((8, wide)), fixed((8, BLOCK)), fixed((1, dv))],
        out_shape=[
            jax.ShapeDtypeStruct((rows, width), BF),
            jax.ShapeDtypeStruct((8, wide), F32),
            jax.ShapeDtypeStruct((8, BLOCK), F32),
            jax.ShapeDtypeStruct((1, dv), F32),
        ],
        scratch_shapes=[
            pltpu.VMEM((heads * dk, dv), F32),
            pltpu.VMEM((BLOCK + 8, wide), F32),
            pltpu.VMEM((BLOCK + 8, wide), F32),
        ],
        compiler_params=pltpu.CompilerParams(dimension_semantics=("arbitrary",)),
        cost_estimate=pl.CostEstimate(flops=6 * rows * heads * 128 * 128 * 16, bytes_accessed=rows * 40000, transcendentals=0),
    )(proj, proj, taps, hp, gain, out, fresh, inverse, states, d_mixed)


def norm_back(values, rms_inv, gain, d_normed):
    scaled = d_normed * gain
    gain_grad = jnp.sum(d_normed * values * rms_inv, 0)
    d_values = rms_inv * scaled - values * rms_inv**3 * jnp.mean(scaled * values, -1, keepdims=True)
    return (d_values, gain_grad)


def weight_grad(source, d_target):
    return jnp.einsum("td,te->de", source, d_target, preferred_element_type=jnp.float32)


def back_product(d_target, weight):
    return jnp.einsum("te,de->td", d_target, weight, preferred_element_type=jnp.float32)


def body(
    inputs, lengths, loss_mask, teacher, attn_gain, q_weight, k_weight, v_weight, gating_weight,
    alpha_weight, beta_weight, q_conv, k_conv, v_conv, decay_log, decay_bias, out_gain, out_weight,
    ffn_gain, ffn_gate, ffn_up, ffn_down,
):
    seq_count, slot_n, width_n = inputs.shape
    tokens_n = seq_count * slot_n
    share_n = slot_n // lax.axis_size("tensor")
    share_start = lax.axis_index("tensor") * share_n
    share_rows = seq_count * share_n
    heads = decay_log.shape[0]
    hk = q_conv.shape[1]
    hv = v_conv.shape[1]
    dk, dv = hk // heads, hv // heads
    wide = 2 * hk + hv
    unit_n = ffn_gate.shape[1]
    local_d = q_weight.shape[0]

    positions = lax.broadcasted_iota(jnp.int32, (seq_count, slot_n), 1)
    valid = (positions < lengths[:, None]).astype(jnp.float32)
    tok_weight = valid * loss_mask.astype(jnp.float32)
    count_all = lax.psum(jnp.sum(tok_weight), "dp")

    spare = BLOCK - 2 * heads - 2
    packed = jnp.concatenate(
        [q_weight, k_weight, v_weight, gating_weight, alpha_weight, beta_weight,
         attn_gain[:, None], ffn_gain[:, None], jnp.zeros((local_d, spare), BF)], 1)
    proj_w = lax.all_gather(packed, "dp", axis=0, tiled=True)
    out_w = lax.all_gather(out_weight, "dp", axis=1, tiled=True)
    pair_w = lax.all_gather(jnp.concatenate([ffn_gate, ffn_up], 1), "dp", axis=0, tiled=True)
    down_w = lax.all_gather(ffn_down, "dp", axis=1, tiled=True)
    gain_at = wide + hv + 2 * heads
    gain_attn = proj_w[:, gain_at].astype(jnp.float32)
    gain_ffn = proj_w[:, gain_at + 1].astype(jnp.float32)

    flat_in = inputs.reshape(tokens_n, width_n).astype(jnp.float32)
    attn_rms = lax.rsqrt(jnp.mean(flat_in * flat_in, -1, keepdims=True) + 1e-06)
    normed = (flat_in * attn_rms * gain_attn).astype(BF)
    proj = jnp.dot(normed, proj_w, preferred_element_type=jnp.float32)
    taps = jnp.pad(jnp.concatenate([q_conv, k_conv, v_conv], 1), ((0, 4), (0, 0)))
    hp = jnp.zeros((8, BLOCK), jnp.float32).at[0, :heads].set(-jnp.exp(decay_log)).at[1, :heads].set(decay_bias)
    mixed_low, mix_out, fresh, inverse, states = delta_forward(proj, taps, hp, out_gain[None], heads, dk, dv)
    attn_part = jnp.dot(mixed_low, out_w, preferred_element_type=jnp.float32).astype(BF)

    def share_of(array):
        return lax.dynamic_slice_in_dim(array, share_start, share_n, 1)

    def scatter_rows(array):
        return lax.psum_scatter(array, "tensor", scatter_dimension=0, tiled=True).astype(jnp.float32)

    def gather_rows(array):
        return lax.all_gather(array, "tensor", axis=0, tiled=True)

    base_in = share_of(inputs).reshape(share_rows, width_n).astype(jnp.float32)
    base_rms = lax.rsqrt(jnp.mean(base_in * base_in, -1, keepdims=True) + 1e-06)
    row_weight = share_of(tok_weight).reshape(share_rows, 1)
    row_valid = share_of(valid).reshape(share_rows, 1)
    row_teacher = share_of(teacher).reshape(share_rows, width_n).astype(jnp.float32)
    resid = base_in + scatter_rows(attn_part)
    ffn_rms = lax.rsqrt(jnp.mean(resid * resid, -1, keepdims=True) + 1e-06)
    normed_ffn = gather_rows((resid * ffn_rms * gain_ffn).astype(BF))
    pre = jnp.dot(normed_ffn, pair_w, preferred_element_type=jnp.float32)
    gate_pre, up_pre = pre[:, :unit_n], pre[:, unit_n:]
    sig_gate = jax.nn.sigmoid(gate_pre)
    silu_gate = gate_pre * sig_gate
    hidden = (silu_gate * up_pre).astype(BF)
    ffn_part = jnp.dot(hidden, down_w, preferred_element_type=jnp.float32).astype(BF)
    output = resid + scatter_rows(ffn_part)
    error = (output - row_teacher) * row_weight
    coef = 0.5 * tokens_n * lax.axis_size("dp") / count_all
    d_output = 2.0 * coef * error * row_weight
    d_ffn = gather_rows(d_output.astype(BF))
    down_grad = weight_grad(hidden, d_ffn).astype(BF)
    d_hidden = back_product(d_ffn, down_w)
    d_gate = (d_hidden * up_pre * sig_gate * (1.0 + gate_pre * (1.0 - sig_gate))).astype(BF)
    d_up = (d_hidden * silu_gate).astype(BF)
    d_pair = jnp.concatenate([d_gate, d_up], 1)
    pair_grad = weight_grad(normed_ffn, d_pair).astype(BF)
    d_nffn = scatter_rows(back_product(d_pair, pair_w).astype(BF))
    d_resid_norm, ffn_gain_grad = norm_back(resid, ffn_rms, gain_ffn, d_nffn)
    d_resid = d_output + d_resid_norm
    d_attn = gather_rows(d_resid.astype(BF))
    out_grad = weight_grad(mixed_low, d_attn).astype(BF)
    d_mixed = back_product(d_attn, out_w).astype(BF)
    d_proj, tap_grad, hp_grad, out_gain_part = delta_backward(
        proj, taps, hp, out_gain[None], mix_out, fresh, inverse, states, d_mixed, heads, dk, dv)
    proj_grad = weight_grad(normed, d_proj).astype(BF)
    d_norm = scatter_rows(back_product(d_proj, proj_w).astype(BF))
    d_in_norm, attn_gain_grad = norm_back(base_in, base_rms, gain_attn, d_norm)
    input_grad = (d_resid + d_in_norm).reshape(seq_count, share_n, width_n)
    activations = (output * row_valid).astype(BF).reshape(seq_count, share_n, width_n)

    down_sum = lax.psum_scatter(down_grad, "dp", scatter_dimension=1, tiled=True).astype(jnp.float32)
    pair_sum = lax.psum_scatter(pair_grad, "dp", scatter_dimension=0, tiled=True).astype(jnp.float32)
    out_sum = lax.psum_scatter(out_grad, "dp", scatter_dimension=1, tiled=True).astype(jnp.float32)
    proj_sum = lax.psum_scatter(proj_grad, "dp", scatter_dimension=0, tiled=True).astype(jnp.float32)

    error_all, gains_all, out_gain_sum = lax.psum(
        (jnp.sum(error * error), jnp.concatenate([attn_gain_grad, ffn_gain_grad]), out_gain_part[0]), ("dp", "tensor"))
    loss = error_all / count_all
    gain_len = width_n // lax.axis_size("dp")
    gain_start = lax.axis_index("dp") * gain_len
    attn_gain_out = lax.dynamic_slice_in_dim(gains_all, gain_start, gain_len, 0)
    ffn_gain_out = lax.dynamic_slice_in_dim(gains_all, width_n + gain_start, gain_len, 0)
    small = jnp.concatenate([tap_grad[:4], jnp.pad(hp_grad[:4], ((0, 0), (0, 0)))], 1)
    small = lax.psum(small, "dp")
    return (
        activations, loss, input_grad, attn_gain_out,
        proj_sum[:, :hk], proj_sum[:, hk : 2 * hk], proj_sum[:, 2 * hk : wide], proj_sum[:, wide : wide + hv],
        proj_sum[:, wide + hv : wide + hv + heads], proj_sum[:, wide + hv + heads : wide + hv + 2 * heads],
        small[:, :hk], small[:, hk : 2 * hk], small[:, 2 * hk : wide],
        small[0, wide : wide + heads], small[1, wide : wide + heads], out_gain_sum,
        out_sum, ffn_gain_out, pair_sum[:, :unit_n], pair_sum[:, unit_n:], down_sum,
    )


def solution(mesh):
    both = P("dp", "tensor")
    rows = P("dp", "tensor", None)
    flip = P("tensor", "dp")
    taps = P(None, "tensor")
    return jax.shard_map(
        body,
        mesh=mesh,
        in_specs=(
            P("dp", None, None), P("dp"), P("dp", None), P("dp", None, None), P("dp"),
            both, both, both, both, both, both, taps, taps, taps,
            P("tensor"), P("tensor"), P(), flip, P("dp"), both, both, flip,
        ),
        out_specs=(
            rows, P(), rows, P("dp"), both, both, both, both, both, both,
            taps, taps, taps, P("tensor"), P("tensor"), P(), flip, P("dp"), both, both, flip,
        ),
        check_vma=False,
    )
```

```python
import functools
import jax
import jax.numpy as jnp
from jax import lax
from jax.experimental import pallas as pl
from jax.experimental.pallas import tpu as pltpu
from jax.sharding import PartitionSpec as P

BLOCK = 128
BF = jnp.bfloat16
F32 = jnp.float32


def mm(a, b, dims=((1,), (0,))):
    return lax.dot_general(a.astype(BF), b.astype(BF), (dims, ((), ())), preferred_element_type=F32)


def mm_nt(a, b):
    return mm(a, b, ((1,), (1,)))


def mm_tn(a, b):
    return mm(a, b, ((0,), (0,)))


def split(a):
    high = a.astype(BF)
    return high, (a - high.astype(F32)).astype(BF)


def mm3(a, b):
    ah, al = a
    bh, bl = b
    return mm(ah, bh) + (mm(ah, bl) + mm(al, bh))


def exact(a, b):
    return lax.dot_general(a, b, (((1,), (0,)), ((), ())), precision=lax.Precision.HIGHEST, preferred_element_type=F32)


def indices():
    rows = lax.broadcasted_iota(jnp.int32, (BLOCK, BLOCK), 0)
    cols = lax.broadcasted_iota(jnp.int32, (BLOCK, BLOCK), 1)
    return rows, cols


def unit_lower_inverse(strict, rows, cols):
    near = jnp.where((rows // 8) == (cols // 8), strict, 0.0)
    eye = (rows == cols).astype(F32)
    first = split(-near)
    second = mm3(first, first)
    second_s = split(second)
    fourth_s = split(mm3(second_s, second_s))
    total = eye - near
    total = total + mm3(split(total), second_s)
    total = total + mm3(split(total), fourth_s)
    size = 8
    while size < BLOCK:
        pick = ((rows // size) == (cols // size) + 1) & ((rows // size) % 2 == 1)
        lower = split(jnp.where(pick, strict, 0.0))
        total_s = split(total)
        total = total - mm3(total_s, split(mm3(lower, total_s)))
        size *= 2
    return total


def decay_terms(ab, hp, rows, cols):
    shifted = ab + hp[1:2, :]
    soft = jnp.maximum(shifted, 0.0) + jnp.log1p(jnp.exp(-jnp.abs(shifted)))
    decay = hp[0:1, :] * soft
    lower = (rows >= cols).astype(F32)
    cum = exact(lower, decay)
    return shifted, decay, cum


def conv_silu(ext_ref, taps, start, width):
    cols = slice(start, start + width)
    total = ext_ref[5 : 5 + BLOCK, cols] * taps[0:1, cols]
    for tap in range(1, 4):
        total = total + ext_ref[5 + tap : 5 + tap + BLOCK, cols] * taps[tap : tap + 1, cols]
    sig = jax.nn.sigmoid(total)
    return total, sig


def forward_kernel(
    heads, dk, dv, n, grid_n, ring_spec, proj_ref, taps_ref, hp_ref, gain_ref, shard_a, shard_b,
    mixed_ref, o_ref, f_ref, t_ref, s_ref, whole_a, whole_b, state, ext, *sems,
):
    hk, hv = heads * dk, heads * dv
    wide = 2 * hk + hv
    ring = RingGather(n, *ring_spec, (shard_a, shard_b), (whole_a, whole_b), sems)
    hosted(ring, n, grid_n)

    @pl.when(pl.program_id(0) == 0)
    def _():
        state[...] = jnp.zeros_like(state)
        ext[0:8, :] = jnp.zeros((8, wide), F32)

    @pl.when(pl.program_id(0) > 0)
    def _():
        ext[0:8, :] = ext[BLOCK : BLOCK + 8, :]

    ext[8 : 8 + BLOCK, :] = proj_ref[:, 0:wide].astype(F32)
    rows, cols = indices()
    ab = proj_ref[:, wide + hv :].astype(F32)
    _, _, cum = decay_terms(ab, hp_ref[...], rows, cols)
    beta_all = jax.nn.sigmoid(ab)
    cum_t = cum.T
    within = rows >= cols
    strict = rows > cols
    taps = taps_ref[...]
    gain = gain_ref[...]
    s_ref[0] = state[...].astype(s_ref.dtype)
    for h in range(heads):
        raw, sig = conv_silu(ext, taps, h * dk, dk)
        act = raw * sig
        query = act * (lax.rsqrt(jnp.sum(act * act, -1, keepdims=True) + 1e-06) * dk ** (-0.5))
        raw, sig = conv_silu(ext, taps, hk + h * dk, dk)
        act = raw * sig
        key = act * lax.rsqrt(jnp.sum(act * act, -1, keepdims=True) + 1e-06)
        raw, sig = conv_silu(ext, taps, 2 * hk + h * dv, dv)
        value = raw * sig
        beta = beta_all[:, heads + h : heads + h + 1]
        c_col = cum[:, h : h + 1]
        c_row = cum_t[h : h + 1, :]
        c_last = cum[BLOCK - 1 : BLOCK, h : h + 1]
        fade = jnp.exp(jnp.where(within, c_col - c_row, 0.0))
        key_b = key.astype(BF)
        query_b = query.astype(BF)
        mix = jnp.where(strict, mm_nt(key_b, key_b) * fade * beta, 0.0)
        inverse = unit_lower_inverse(mix, rows, cols)
        inv_b = inverse.astype(BF)
        t_ref[:, h * BLOCK : (h + 1) * BLOCK] = inv_b
        grow = jnp.exp(c_col)
        w_rows = mm(inv_b, key * (beta * grow))
        u_rows = mm(inv_b, value * beta)
        memory = state[h * dk : (h + 1) * dk, :]
        mem_b = memory.astype(BF)
        fresh = u_rows - mm(w_rows, mem_b)
        fresh_b = fresh.astype(BF)
        f_ref[:, h * dv : (h + 1) * dv] = fresh_b
        scores = jnp.where(within, mm_nt(query_b, key_b) * fade, 0.0)
        out = mm(query_b, mem_b) * grow + mm(scores, fresh_b)
        state[h * dk : (h + 1) * dk, :] = jnp.exp(c_last) * memory + mm_tn(
            key * jnp.exp(c_last - c_col), fresh_b
        )
        o_ref[:, h * dv : (h + 1) * dv] = out.astype(o_ref.dtype)
        gate = proj_ref[:, wide + h * dv : wide + (h + 1) * dv].astype(F32)
        scale = lax.rsqrt(jnp.mean(out * out, -1, keepdims=True) + 1e-05)
        mixed_ref[:, h * dv : (h + 1) * dv] = (
            out * scale * gain * (gate * jax.nn.sigmoid(gate))
        ).astype(mixed_ref.dtype)

    @pl.when(pl.program_id(0) == grid_n - 1)
    def _():
        ring.finish()


def delta_forward(proj, taps, hp, gain, shards, kinds, n, heads, dk, dv, store=BF):
    ring_spec = ([s.shape for s in shards], kinds, (2, 2))
    rows = proj.shape[0]
    steps = rows // BLOCK
    wide = 2 * heads * dk + heads * dv
    width = proj.shape[1]
    hv = heads * dv

    def by_step(cols):
        return pl.BlockSpec((BLOCK, cols), lambda i: (i, 0))

    def fixed(shape):
        return pl.BlockSpec(shape, lambda i: (0, 0))

    return pl.pallas_call(
        functools.partial(forward_kernel, heads, dk, dv, n, steps, ring_spec),
        grid=(steps,),
        in_specs=[by_step(width), fixed(taps.shape), fixed(hp.shape), fixed(gain.shape), ANYWHERE, ANYWHERE],
        out_specs=[
            by_step(hv), by_step(hv), by_step(hv), by_step(heads * BLOCK),
            pl.BlockSpec((1, heads * dk, dv), lambda i: (i, 0, 0)),
            ANYWHERE, ANYWHERE,
        ],
        out_shape=[
            jax.ShapeDtypeStruct((rows, hv), BF),
            jax.ShapeDtypeStruct((rows, hv), store),
            jax.ShapeDtypeStruct((rows, hv), BF),
            jax.ShapeDtypeStruct((rows, heads * BLOCK), BF),
            jax.ShapeDtypeStruct((steps, heads * dk, dv), BF),
            *[jax.ShapeDtypeStruct(whole_shape(n, s.shape, k), BF) for s, k in zip(shards, kinds)],
        ],
        scratch_shapes=[
            pltpu.VMEM((heads * dk, dv), F32),
            pltpu.VMEM((BLOCK + 8, wide), F32),
            *RingGather.scratch(n, ring_spec[0], ring_spec[2]),
        ],
        compiler_params=comm_params(2),
        cost_estimate=pl.CostEstimate(flops=6 * rows * heads * 128 * 128 * 10, bytes_accessed=rows * 30000, transcendentals=0),
    )(proj, taps, hp, gain, *shards)


def unit_back(act, scale, grad):
    return scale * grad - act * (scale * scale * scale) * jnp.sum(grad * act, -1, keepdims=True)


def silu_back(raw, sig, grad):
    return grad * (sig * (1.0 + raw * (1.0 - sig)))


def backward_kernel(
    heads, dk, dv, n, grid_n, ring_spec, proj_ref, halo_ref, taps_ref, hp_ref, gain_ref, o_ref, f_ref, t_ref, s_ref,
    dm_ref, grad_a, grad_b, dproj_ref, dtaps_ref, dhp_ref, dgain_ref, sum_a, sum_b, dstate, ext, dext, *scratch,
):
    hk, hv = heads * dk, heads * dv
    wide = 2 * hk + hv
    ring = RingScatter(n, *ring_spec, (grad_a, grad_b), (sum_a, sum_b), scratch)
    hosted(ring, n, grid_n)
    step = pl.program_id(0)
    last = pl.num_programs(0) - 1

    @pl.when(step == 0)
    def _():
        dstate[...] = jnp.zeros_like(dstate)
        dext[BLOCK : BLOCK + 8, :] = jnp.zeros((8, wide), F32)
        dtaps_ref[...] = jnp.zeros_like(dtaps_ref)
        dhp_ref[...] = jnp.zeros_like(dhp_ref)
        dgain_ref[...] = jnp.zeros_like(dgain_ref)

    @pl.when(step > 0)
    def _():
        dext[BLOCK : BLOCK + 8, :] = dext[0:8, :]

    ext[0:8, :] = jnp.where(step == last, 0.0, halo_ref[:, 0:wide].astype(F32))
    ext[8 : 8 + BLOCK, :] = proj_ref[:, 0:wide].astype(F32)
    rows, cols = indices()
    ab = proj_ref[:, wide + hv :].astype(F32)
    hp = hp_ref[...]
    shifted, decay, cum = decay_terms(ab, hp, rows, cols)
    beta_all = jax.nn.sigmoid(ab)
    cum_t = cum.T
    within = rows >= cols
    strict = rows > cols
    taps = taps_ref[...]
    gain = gain_ref[...]
    lane = cols
    dbeta_all = jnp.zeros((BLOCK, BLOCK), F32)
    dcum_all = jnp.zeros((BLOCK, BLOCK), F32)
    dcum_rows = jnp.zeros((BLOCK, BLOCK), F32)
    dlast_all = jnp.zeros((1, BLOCK), F32)
    dgain = jnp.zeros((1, dv), F32)
    for h in range(heads):
        q_cols = slice(h * dk, (h + 1) * dk)
        k_cols = slice(hk + h * dk, hk + (h + 1) * dk)
        v_cols = slice(2 * hk + h * dv, 2 * hk + (h + 1) * dv)
        o_cols = slice(h * dv, (h + 1) * dv)
        gate = proj_ref[:, wide + h * dv : wide + (h + 1) * dv].astype(F32)
        out = o_ref[:, o_cols].astype(F32)
        d_mixed = dm_ref[:, o_cols].astype(F32)
        scale = lax.rsqrt(jnp.mean(out * out, -1, keepdims=True) + 1e-05)
        sig = jax.nn.sigmoid(gate)
        base = out * scale * d_mixed
        dgain = dgain + jnp.sum(base * (gate * sig), 0, keepdims=True)
        dproj_ref[:, wide + h * dv : wide + (h + 1) * dv] = silu_back(gate, sig, base * gain).astype(dproj_ref.dtype)
        d_normed = d_mixed * gain * (gate * sig)
        d_out = scale * d_normed - out * (scale * scale * scale) * jnp.mean(d_normed * out, -1, keepdims=True)
        d_out_b = d_out.astype(BF)
        q_raw, q_sig = conv_silu(ext, taps, h * dk, dk)
        q_act = q_raw * q_sig
        q_scale = lax.rsqrt(jnp.sum(q_act * q_act, -1, keepdims=True) + 1e-06)
        query = q_act * (q_scale * dk ** (-0.5))
        k_raw, k_sig = conv_silu(ext, taps, hk + h * dk, dk)
        k_act = k_raw * k_sig
        k_scale = lax.rsqrt(jnp.sum(k_act * k_act, -1, keepdims=True) + 1e-06)
        key = k_act * k_scale
        v_raw, v_sig = conv_silu(ext, taps, 2 * hk + h * dv, dv)
        value = v_raw * v_sig
        beta = beta_all[:, heads + h : heads + h + 1]
        c_col = cum[:, h : h + 1]
        c_row = cum_t[h : h + 1, :]
        c_last = cum[BLOCK - 1 : BLOCK, h : h + 1]
        fade = jnp.exp(jnp.where(within, c_col - c_row, 0.0))
        key_b = key.astype(BF)
        query_b = query.astype(BF)
        grow = jnp.exp(c_col)
        rest = jnp.exp(c_last - c_col)
        kk = jnp.where(strict, mm_nt(key_b, key_b) * fade, 0.0)
        scores = jnp.where(within, mm_nt(query_b, key_b) * fade, 0.0)
        inv_b = t_ref[:, h * BLOCK : (h + 1) * BLOCK]
        fresh_b = f_ref[:, o_cols]
        mem_b = s_ref[0, h * dk : (h + 1) * dk, :]
        d_mem = dstate[h * dk : (h + 1) * dk, :]
        d_mem_b = d_mem.astype(BF)
        d_fresh = mm_tn(scores, d_out_b) + mm(key * rest, d_mem_b)
        d_right = mm_tn(inv_b, d_fresh)
        d_right_b = d_right.astype(BF)
        d_scores = jnp.where(within, mm_nt(d_out_b, fresh_b), 0.0)
        d_mix = jnp.where(strict, -mm_nt(d_right_b, fresh_b), 0.0)
        x_rows = mm_nt(d_right_b, mem_b)
        y_rows = mm_nt(d_out_b, mem_b)
        z_rows = mm_nt(fresh_b, d_mem_b)
        decay_all = jnp.exp(c_last)
        dstate[h * dk : (h + 1) * dk, :] = (
            decay_all * d_mem
            + mm_tn(query * grow, d_out_b)
            - mm_tn(key * (beta * grow), d_right_b)
        )
        x_sum = jnp.sum(x_rows * key, -1, keepdims=True)
        y_sum = jnp.sum(y_rows * query, -1, keepdims=True)
        z_sum = jnp.sum(z_rows * key, -1, keepdims=True) * rest
        mix_part = d_mix * kk
        d_beta = (
            jnp.sum(d_right * value, -1, keepdims=True)
            - grow * x_sum
            + jnp.sum(mix_part, -1, keepdims=True)
        )
        pair = d_scores * scores + mix_part * beta
        d_cum = jnp.sum(pair, -1, keepdims=True) + grow * (y_sum - beta * x_sum) - z_sum
        d_last = jnp.sum(z_sum, 0, keepdims=True) + decay_all * jnp.sum(
            jnp.sum(d_mem * mem_b.astype(F32), -1, keepdims=True), 0, keepdims=True
        )
        dbeta_all = jnp.where(lane == heads + h, d_beta, dbeta_all)
        dcum_all = jnp.where(lane == h, d_cum, dcum_all)
        dcum_rows = jnp.where(rows == h, jnp.sum(pair, 0, keepdims=True), dcum_rows)
        dlast_all = jnp.where(lane[0:1, :] == h, d_last, dlast_all)
        g_scores = (d_scores * fade).astype(BF)
        g_mix = (d_mix * fade * beta).astype(BF)
        d_query = grow * y_rows + mm(g_scores, key_b)
        d_key = (
            rest * z_rows - (beta * grow) * x_rows
            + mm_tn(g_scores, query_b) + mm(g_mix, key_b) + mm_tn(g_mix, key_b)
        )
        d_value = d_right * beta
        dext[0:BLOCK, q_cols] = silu_back(q_raw, q_sig, unit_back(q_act, q_scale, d_query * dk ** (-0.5)))
        dext[0:BLOCK, k_cols] = silu_back(k_raw, k_sig, unit_back(k_act, k_scale, d_key))
        dext[0:BLOCK, v_cols] = silu_back(v_raw, v_sig, d_value)
    dgain_ref[...] += dgain
    d_cum = dcum_all - dcum_rows.T + jnp.where(rows == BLOCK - 1, dlast_all, 0.0)
    upper = (rows <= cols).astype(F32)
    d_decay = exact(upper, d_cum)
    d_alpha = d_decay * hp[0:1, :] * jax.nn.sigmoid(shifted)
    d_ab = d_alpha + dbeta_all * beta_all * (1.0 - beta_all)
    dproj_ref[:, wide + hv :] = d_ab.astype(dproj_ref.dtype)
    dhp_ref[0:1, :] += jnp.sum(d_decay * decay, 0, keepdims=True)
    dhp_ref[1:2, :] += jnp.sum(d_alpha, 0, keepdims=True)
    chunk = 256
    for start in range(0, wide, chunk):
        part = slice(start, start + chunk)
        d_conv = dext[0:BLOCK, part]
        total = dext[3 : 3 + BLOCK, part] * taps[0:1, part]
        dtaps_ref[0:1, part] += jnp.sum(d_conv * ext[5 : 5 + BLOCK, part], 0, keepdims=True)
        for tap in range(1, 4):
            total = total + dext[3 - tap : 3 - tap + BLOCK, part] * taps[tap : tap + 1, part]
            dtaps_ref[tap : tap + 1, part] += jnp.sum(d_conv * ext[5 + tap : 5 + tap + BLOCK, part], 0, keepdims=True)
        dproj_ref[:, part] = total.astype(dproj_ref.dtype)

    @pl.when(step == grid_n - 1)
    def _():
        ring.finish()


def delta_backward(
    proj, taps, hp, gain, out, fresh, inverse, states, d_mixed, grads, shapes, kinds, n, heads, dk, dv,
):
    ring_spec = (shapes, kinds, (2, 2))
    rows, width = proj.shape
    steps = rows // BLOCK
    wide = 2 * heads * dk + heads * dv
    hv = heads * dv

    def by_step(cols):
        return pl.BlockSpec((BLOCK, cols), lambda i: (steps - 1 - i, 0))

    def fixed(shape):
        return pl.BlockSpec(shape, lambda i: (0, 0))

    per = BLOCK // 8
    return pl.pallas_call(
        functools.partial(backward_kernel, heads, dk, dv, n, steps, ring_spec),
        grid=(steps,),
        in_specs=[
            by_step(width),
            pl.BlockSpec((8, width), lambda i: (jnp.maximum((steps - 1 - i) * per - 1, 0), 0)),
            fixed(taps.shape), fixed(hp.shape), fixed(gain.shape),
            by_step(hv), by_step(hv), by_step(heads * BLOCK),
            pl.BlockSpec((1, heads * dk, dv), lambda i: (steps - 1 - i, 0, 0)),
            by_step(hv), ANYWHERE, ANYWHERE,
        ],
        out_specs=[
            by_step(width), fixed((8, wide)), fixed((8, BLOCK)), fixed((1, dv)), *[fixed(s) for s in shapes],
        ],
        out_shape=[
            jax.ShapeDtypeStruct((rows, width), BF),
            jax.ShapeDtypeStruct((8, wide), F32),
            jax.ShapeDtypeStruct((8, BLOCK), F32),
            jax.ShapeDtypeStruct((1, dv), F32),
            *[jax.ShapeDtypeStruct(s, F32) for s in shapes],
        ],
        scratch_shapes=[
            pltpu.VMEM((heads * dk, dv), F32),
            pltpu.VMEM((BLOCK + 8, wide), F32),
            pltpu.VMEM((BLOCK + 8, wide), F32),
            *RingScatter.scratch(n, shapes, ring_spec[2]),
        ],
        compiler_params=comm_params(9),
        cost_estimate=pl.CostEstimate(flops=6 * rows * heads * 128 * 128 * 16, bytes_accessed=rows * 40000, transcendentals=0),
    )(proj, proj, taps, hp, gain, out, fresh, inverse, states, d_mixed, *grads)


MESH = pl.DeviceIdType.MESH


def ring_place(index, n):
    half = index // 2
    return half + (index % 2) * (n - 1 - 2 * half)


def ring_index(place, n):
    far = place // (n // 2)
    return (1 - far) * 2 * place + far * (2 * (n - 1 - place) + 1)


class Ring:
    def __init__(self, n, shapes, kinds, parts):
        self.n, self.shapes, self.kinds, self.parts = n, shapes, kinds, parts
        self.place = ring_place(lax.axis_index("dp"), n)
        self.next = ring_index((self.place + 1) % n, n)
        self.prev = ring_index((self.place + n - 1) % n, n)

    def greet(self, barrier):
        for device in (self.next, self.prev):
            pl.semaphore_signal(barrier, inc=1, device_id={"dp": device}, device_id_type=MESH)
        return 2

    def pieces(self):
        stream = 0
        for i, (rows, _) in enumerate(self.shapes):
            size = rows // (2 * self.parts[i])
            for part in range(self.parts[i]):
                for way in range(2):
                    yield stream, i, way, (way * self.parts[i] + part) * size, size
                    stream += 1

    def window(self, ref, i, block, offset, size):
        rows, cols = self.shapes[i]
        if self.kinds[i] == "rows":
            return ref.at[pl.ds(pl.multiple_of(block * rows + offset, 16), size), :]
        if self.kinds[i] == "cols":
            return ref.at[pl.ds(offset, size), pl.ds(pl.multiple_of(block * cols, 128), cols)]
        return ref.at[block, pl.ds(offset, size), :]

    def send(self, source, target, send_sem, recv_sem, way):
        return pltpu.make_async_remote_copy(
            src_ref=source, dst_ref=target, send_sem=send_sem, recv_sem=recv_sem,
            device_id={"dp": self.next if way == 0 else self.prev}, device_id_type=MESH)


def ring_streams(parts):
    return 2 * sum(parts)


class RingGather(Ring):
    def __init__(self, n, shapes, kinds, parts, shards, wholes, sems, starts=None):
        super().__init__(n, shapes, kinds, parts)
        self.shards, self.wholes = shards, wholes
        self.send_sem, self.recv_sem, self.own_sem = sems

    @staticmethod
    def scratch(n, shapes, parts):
        count = ring_streams(parts)
        dma = pltpu.SemaphoreType.DMA
        return [dma((n - 1, count)), dma((n - 1, count)), dma((len(shapes),))]

    def copies(self, step):
        made = []
        for stream, i, way, offset, size in self.pieces():
            ahead = self.n - step if way == 0 else step
            block = ring_index((self.place + ahead) % self.n, self.n)
            there = self.window(self.wholes[i], i, block, offset, size)
            first = isinstance(step, int) and step == 0
            here = self.shards[i].at[pl.ds(offset, size), :] if first else there
            made.append(self.send(here, there, self.send_sem.at[step, stream], self.recv_sem.at[step, stream], way))
        return made

    def own(self):
        me = lax.axis_index("dp")
        return [
            pltpu.make_async_copy(shard, self.window(whole, i, me, 0, self.shapes[i][0]), self.own_sem.at[i])
            for i, (shard, whole) in enumerate(zip(self.shards, self.wholes))
        ]

    def start(self):
        for copy in self.copies(0) + self.own():
            copy.start()

    def step(self, step):
        for old, new in zip(self.copies(step - 1), self.copies(step)):
            old.wait_recv()
            new.start()

    def finish(self):
        for copy in self.copies(self.n - 2):
            copy.wait_recv()

        def done(step, carry):
            for copy in self.copies(step):
                copy.wait_send()
            return carry

        lax.fori_loop(0, self.n - 1, done, 0)
        for copy in self.own():
            copy.wait()


class RingScatter(Ring):
    def __init__(self, n, shapes, kinds, parts, grads, results, scratch):
        super().__init__(n, shapes, kinds, parts)
        count = len(shapes)
        self.grads, self.results = grads, results
        self.slots, self.mine = scratch[:count], scratch[count : 2 * count]
        self.send_sem, self.recv_sem, self.load_sem = scratch[2 * count :]

    @staticmethod
    def scratch(n, shapes, parts):
        count = ring_streams(parts)
        dma = pltpu.SemaphoreType.DMA
        return (
            [pltpu.VMEM((n - 1, rows, cols), BF) for rows, cols in shapes]
            + [pltpu.VMEM((2, rows, cols), BF) for rows, cols in shapes]
            + [dma((n - 1, count)), dma((n - 1, count)), dma((2, count))]
        )

    def grad(self, step, i, way, offset, size):
        ahead = 2 * self.n - 1 - step if way == 0 else 1 + step
        block = ring_index((self.place + ahead) % self.n, self.n)
        return self.window(self.grads[i], i, block, offset, size)

    def copy(self, step, piece):
        stream, i, way, offset, size = piece
        rows = pl.ds(offset, size)
        if isinstance(step, int) and step == 0:
            here = self.grad(0, i, way, offset, size)
        else:
            here = self.slots[i].at[step - 1, rows, :]
        return self.send(
            here, self.slots[i].at[step, rows, :], self.send_sem.at[step, stream], self.recv_sem.at[step, stream], way)

    def arrival(self, step, piece):
        stream, i, way, offset, size = piece
        slot = self.slots[i].at[step, pl.ds(offset, size), :]
        return self.send(slot, slot, self.send_sem.at[step, stream], self.recv_sem.at[step, stream], way)

    def load(self, step, piece):
        stream, i, way, offset, size = piece
        half = step % 2
        return pltpu.make_async_copy(
            self.grad(step, i, way, offset, size), self.mine[i].at[half, pl.ds(offset, size), :],
            self.load_sem.at[half, stream])

    def start(self):
        for piece in self.pieces():
            self.copy(0, piece).start()
        for piece in self.pieces():
            self.load(1, piece).start()

    def add(self, step, piece, store):
        _, i, _, offset, size = piece
        high = 16

        def rows(k, carry):
            at = pl.ds(pl.multiple_of(offset + k * high, high), high)
            total = self.slots[i][step - 1, at, :].astype(F32) + self.mine[i][step % 2, at, :].astype(F32)
            store(i, at, total)
            return carry

        lax.fori_loop(0, size // high, rows, 0)

    def step(self, step):
        for piece in self.pieces():
            self.load(step + 1, piece).start()
        for piece in self.pieces():
            self.arrival(step - 1, piece).wait_recv()
            self.load(step, piece).wait()

            def store(i, at, total):
                self.slots[i][step - 1, at, :] = total.astype(BF)

            self.add(step, piece, store)
            self.copy(step, piece).start()

    def finish(self):
        last = self.n - 1
        for piece in self.pieces():
            self.arrival(last - 1, piece).wait_recv()
            self.load(last, piece).wait()

            def store(i, at, total):
                self.results[i][at, :] = total

            self.add(last, piece, store)

        def done(step, carry):
            for piece in self.pieces():
                self.arrival(step, piece).wait_send()
            return carry

        lax.fori_loop(0, self.n - 1, done, 0)


class Quad:
    def __init__(self):
        me = lax.axis_index("tensor")
        self.me = me
        self.near = me + 1 - 2 * (me % 2)
        self.far = (me + 2) % 4
        self.cross = (self.near + 2) % 4

    def greet(self, barrier):
        for device in (self.near, self.far):
            pl.semaphore_signal(barrier, inc=1, device_id={"tensor": device}, device_id_type=MESH)
        return 2

    @staticmethod
    def send(source, target, send_sem, recv_sem, device):
        return pltpu.make_async_remote_copy(
            src_ref=source, dst_ref=target, send_sem=send_sem, recv_sem=recv_sem,
            device_id={"tensor": device}, device_id_type=MESH)


class QuadGather(Quad):
    def __init__(self, rows, parts, shard, whole, sems):
        super().__init__()
        self.rows, self.parts, self.shard, self.whole = rows, parts, shard, whole
        self.send_sem, self.recv_sem, self.own_sem = sems

    @staticmethod
    def scratch(parts):
        dma = pltpu.SemaphoreType.DMA
        return [dma((3, parts)), dma((3, parts)), dma((1,))]

    def at(self, block, part):
        size = self.rows // self.parts
        return self.whole.at[pl.ds(pl.multiple_of(block * self.rows + part * size, 16), size), :]

    def copy(self, kind, part):
        size = self.rows // self.parts
        here = self.shard.at[pl.ds(part * size, size), :]
        sems = (self.send_sem.at[kind, part], self.recv_sem.at[kind, part])
        if kind == 0:
            return self.send(here, self.at(self.me, part), *sems, self.far)
        if kind == 1:
            return self.send(here, self.at(self.me, part), *sems, self.near)
        return self.send(self.at(self.far, part), self.at(self.far, part), *sems, self.near)

    def own(self):
        return pltpu.make_async_copy(
            self.shard, self.whole.at[pl.ds(pl.multiple_of(self.me * self.rows, 16), self.rows), :], self.own_sem.at[0])

    def start(self):
        for part in range(self.parts):
            self.copy(0, part).start()
        for part in range(self.parts):
            self.copy(1, part).start()
        self.own().start()

    def step(self, part):
        self.copy(0, part).wait_recv()
        self.copy(2, part).start()

    def finish(self):
        for part in range(self.parts):
            self.copy(1, part).wait_recv()
            self.copy(2, part).wait_recv()
            for kind in range(3):
                self.copy(kind, part).wait_send()
        self.own().wait()


class QuadScatter(Quad):
    def __init__(self, rows, parts, partial, result, scratch):
        super().__init__()
        self.rows, self.parts, self.partial, self.result = rows, parts, partial, result
        self.pair, self.mine, self.other, self.send_sem, self.recv_sem, self.load_sem = scratch

    @staticmethod
    def scratch(rows, cols, parts):
        dma = pltpu.SemaphoreType.DMA
        return [
            pltpu.VMEM((2, rows, cols), BF), pltpu.VMEM((2, rows, cols), BF), pltpu.VMEM((rows, cols), BF),
            dma((3, parts)), dma((3, parts)), dma((2, parts)),
        ]

    def part_rows(self, part):
        size = self.rows // self.parts
        return pl.ds(part * size, size)

    def at(self, block, part):
        size = self.rows // self.parts
        return self.partial.at[pl.ds(pl.multiple_of(block * self.rows + part * size, 16), size), :]

    def copy(self, kind, part):
        rows = self.part_rows(part)
        sems = (self.send_sem.at[kind, part], self.recv_sem.at[kind, part])
        if kind == 0:
            return self.send(self.at(self.cross, part), self.pair.at[0, rows, :], *sems, self.near)
        if kind == 1:
            return self.send(self.at(self.near, part), self.pair.at[1, rows, :], *sems, self.near)
        return self.send(self.pair.at[0, rows, :], self.other.at[rows, :], *sems, self.far)

    def load(self, kind, part):
        block = self.far if kind == 0 else self.me
        return pltpu.make_async_copy(
            self.at(block, part), self.mine.at[kind, self.part_rows(part), :], self.load_sem.at[kind, part])

    def start(self):
        for kind in range(2):
            for part in range(self.parts):
                self.copy(kind, part).start()
                self.load(kind, part).start()

    def over(self, part, work):
        size = self.rows // self.parts
        high = 16

        def rows(k, carry):
            work(pl.ds(pl.multiple_of(part * size + k * high, high), high))
            return carry

        lax.fori_loop(0, size // high, rows, 0)

    def step(self, part):
        self.copy(0, part).wait_recv()
        self.load(0, part).wait()

        def work(at):
            total = self.pair[0, at, :].astype(F32) + self.mine[0, at, :].astype(F32)
            self.pair[0, at, :] = total.astype(BF)

        self.over(part, work)
        self.copy(2, part).start()

    def finish(self):
        for part in range(self.parts):
            self.copy(1, part).wait_recv()
            self.load(1, part).wait()
            self.copy(2, part).wait_recv()

            def work(at):
                near = self.pair[1, at, :].astype(F32) + self.mine[1, at, :].astype(F32)
                self.result[at, :] = near + self.other[at, :].astype(F32)

            self.over(part, work)
        for part in range(self.parts):
            for kind in range(3):
                self.copy(kind, part).wait_send()


def meet(*groups):
    barrier = pltpu.get_barrier_semaphore()
    pl.semaphore_wait(barrier, sum(group.greet(barrier) for group in groups))


def run_between(ring, first, stop):
    def body(step, carry):
        ring.step(step)
        return carry

    lax.fori_loop(first, stop, body, 0)


def interleave(ring, quad, n):
    total = n - 2
    for part in range(quad.parts):
        quad.step(part)
        run_between(ring, 1 + total * part // quad.parts, 1 + total * (part + 1) // quad.parts)


def hosted(ring, n, grid_n):
    here = pl.program_id(0)

    @pl.when(here == 0)
    def _():
        meet(ring)
        ring.start()

    per = (n - 2 + grid_n - 3) // (grid_n - 2)

    @pl.when((here > 0) & (here < grid_n - 1))
    def _():
        run_between(ring, jnp.minimum(1 + (here - 1) * per, n - 1), jnp.minimum(1 + here * per, n - 1))


def whole_shape(n, shape, kind):
    rows, cols = shape
    if kind == "rows":
        return (n * rows, cols)
    if kind == "cols":
        return (rows, n * cols)
    return (n, rows, cols)


ANYWHERE = pl.BlockSpec(memory_space=pl.ANY)
IN_VMEM = pl.BlockSpec(memory_space=pltpu.VMEM)


def comm_params(collective_id):
    return pltpu.CompilerParams(collective_id=collective_id, has_side_effects=True)


class Spread:
    def __init__(self, axis, n, mine, box, sems):
        self.axis, self.n, self.mine, self.box = axis, n, mine, box
        self.send_sem, self.recv_sem = sems
        self.me = lax.axis_index(axis)

    @staticmethod
    def scratch(n, shape):
        dma = pltpu.SemaphoreType.DMA
        return [pltpu.VMEM((n, *shape), F32), dma((n - 1,)), dma((n - 1,))]

    def greet(self, barrier):
        def one(off, carry):
            device = (self.me + off) % self.n
            pl.semaphore_signal(barrier, inc=1, device_id={self.axis: device}, device_id_type=MESH)
            return carry

        lax.fori_loop(1, self.n, one, 0)
        return self.n - 1

    def copy(self, off):
        return pltpu.make_async_remote_copy(
            src_ref=self.mine, dst_ref=self.box.at[self.me], send_sem=self.send_sem.at[off - 1],
            recv_sem=self.recv_sem.at[off - 1], device_id={self.axis: (self.me + off) % self.n}, device_id_type=MESH)

    def arrival(self, off):
        slot = self.box.at[(self.me + self.n - off) % self.n]
        return pltpu.make_async_remote_copy(
            src_ref=self.mine, dst_ref=slot, send_sem=self.send_sem.at[off - 1],
            recv_sem=self.recv_sem.at[off - 1], device_id={self.axis: (self.me + off) % self.n}, device_id_type=MESH)

    def start(self):
        def one(off, carry):
            self.copy(off).start()
            return carry

        lax.fori_loop(1, self.n, one, 0)
        self.box[self.me] = self.mine[...]

    def total(self):
        def one(off, carry):
            self.arrival(off).wait_recv()
            self.copy(off).wait_send()
            return carry

        lax.fori_loop(1, self.n, one, 0)
        return lax.fori_loop(1, self.n, lambda j, carry: carry + self.box[j], self.box[0])


def first_kernel(n, spec, shard_a, shard_b, count_ref, whole_a, whole_b, total_ref, *scratch):
    ring = RingGather(n, *spec, (shard_a, shard_b), (whole_a, whole_b), scratch[:3])
    spread = Spread("dp", n, count_ref, scratch[3], scratch[4:])
    barrier = pltpu.get_barrier_semaphore()
    pl.semaphore_wait(barrier, spread.greet(barrier))
    spread.start()
    ring.start()
    run_between(ring, 1, n - 1)
    total_ref[...] = spread.total()
    ring.finish()


def gather_first(packed, gains, count, n):
    shards = (packed, gains)
    spec = ([s.shape for s in shards], ("rows", "rows"), (2, 1))
    return pl.pallas_call(
        functools.partial(first_kernel, n, spec),
        in_specs=[ANYWHERE, ANYWHERE, IN_VMEM],
        out_specs=[ANYWHERE, ANYWHERE, IN_VMEM],
        out_shape=[jax.ShapeDtypeStruct(whole_shape(n, s.shape, "rows"), BF) for s in shards]
        + [jax.ShapeDtypeStruct(count.shape, F32)],
        scratch_shapes=RingGather.scratch(n, spec[0], spec[2]) + Spread.scratch(n, count.shape),
        compiler_params=comm_params(1),
    )(packed, gains, count)


def rows_of(ref, kind, start, rows):
    if kind == "cols":
        return ref.at[pl.ds(start, rows), :]
    return ref.at[:, pl.ds(start, rows), :]


def scatter_gather_kernel(n, spec, start, rows, parts, partial, shard, result, whole, *scratch):
    quad = QuadScatter(rows, parts, partial, result, scratch[3:])
    size = spec[0][0][0]
    ring = RingGather(
        n, *spec, (shard.at[pl.ds(start, size), :],), (rows_of(whole, spec[1][0], start, size),), scratch[:3])
    meet(quad, ring)
    quad.start()
    ring.start()
    interleave(ring, quad, n)
    quad.finish()
    ring.finish()


def scatter_and_gather(partial, shard, kind, start, size, n, collective_id, parts=4):
    rows, cols = partial.shape[0] // 4, partial.shape[1]
    spec = ([(size, shard.shape[1])], (kind,), (2,))
    return pl.pallas_call(
        functools.partial(scatter_gather_kernel, n, spec, start, rows, parts),
        in_specs=[ANYWHERE, ANYWHERE],
        out_specs=[IN_VMEM, ANYWHERE],
        out_shape=[
            jax.ShapeDtypeStruct((rows, cols), F32),
            jax.ShapeDtypeStruct(whole_shape(n, shard.shape, kind), BF),
        ],
        scratch_shapes=RingGather.scratch(n, spec[0], spec[2]) + QuadScatter.scratch(rows, cols, parts),
        compiler_params=comm_params(collective_id),
    )(partial, shard)


def gather_gather_kernel(n, spec, start, rows, parts, mine, shard, _, out, whole, *scratch):
    quad = QuadGather(rows, parts, mine, out, scratch[3:])
    size = spec[0][0][0]
    ring = RingGather(
        n, *spec, (shard.at[pl.ds(start, size), :],), (rows_of(whole, spec[1][0], start, size),), scratch[:3])
    meet(quad, ring)
    quad.start()
    ring.start()
    interleave(ring, quad, n)
    quad.finish()
    ring.finish()


def gather_and_gather(mine, shard, whole, kind, start, size, n, collective_id, parts=4):
    rows, cols = mine.shape
    spec = ([(size, shard.shape[1])], (kind,), (2,))
    return pl.pallas_call(
        functools.partial(gather_gather_kernel, n, spec, start, rows, parts),
        in_specs=[ANYWHERE, ANYWHERE, ANYWHERE],
        out_specs=[ANYWHERE, ANYWHERE],
        out_shape=[
            jax.ShapeDtypeStruct((4 * rows, cols), BF),
            jax.ShapeDtypeStruct(whole.shape, BF),
        ],
        input_output_aliases={2: 1},
        scratch_shapes=RingGather.scratch(n, spec[0], spec[2]) + QuadGather.scratch(parts),
        compiler_params=comm_params(collective_id),
    )(mine, shard, whole)


def scatter_kernel(rows, parts, partial, result, *scratch):
    quad = QuadScatter(rows, parts, partial, result, scratch)
    meet(quad)
    quad.start()
    for part in range(parts):
        quad.step(part)
    quad.finish()


def scatter_rows(partial, collective_id, parts=4):
    rows, cols = partial.shape[0] // 4, partial.shape[1]
    return pl.pallas_call(
        functools.partial(scatter_kernel, rows, parts),
        in_specs=[ANYWHERE],
        out_specs=IN_VMEM,
        out_shape=jax.ShapeDtypeStruct((rows, cols), F32),
        scratch_shapes=QuadScatter.scratch(rows, cols, parts),
        compiler_params=comm_params(collective_id),
    )(partial)


def gather_kernel(rows, parts, mine, out, *scratch):
    quad = QuadGather(rows, parts, mine, out, scratch)
    meet(quad)
    quad.start()
    for part in range(parts):
        quad.step(part)
    quad.finish()


def gather_rows(mine, collective_id, parts=4):
    rows, cols = mine.shape
    return pl.pallas_call(
        functools.partial(gather_kernel, rows, parts),
        in_specs=[ANYWHERE],
        out_specs=ANYWHERE,
        out_shape=jax.ShapeDtypeStruct((4 * rows, cols), BF),
        scratch_shapes=QuadGather.scratch(parts),
        compiler_params=comm_params(collective_id),
    )(mine)


def scatter_scatter_kernel(n, spec, start, rows, parts, partial, grad, result, total, *scratch):
    count = len(QuadScatter.scratch(rows, 128, parts))
    quad = QuadScatter(rows, parts, partial, result, scratch[:count])
    ring = RingScatter(n, *spec, (rows_of(grad, spec[1][0], start, spec[0][0][0]),), (total,), scratch[count:])
    meet(quad, ring)
    quad.start()
    ring.start()
    interleave(ring, quad, n)
    quad.finish()
    ring.finish()


def scatter_and_scatter(partial, grad, shape, kind, start, n, collective_id, parts=4):
    rows, cols = partial.shape[0] // 4, partial.shape[1]
    spec = ([shape], (kind,), (2,))
    return pl.pallas_call(
        functools.partial(scatter_scatter_kernel, n, spec, start, rows, parts),
        in_specs=[ANYWHERE, ANYWHERE],
        out_specs=[IN_VMEM, IN_VMEM],
        out_shape=[jax.ShapeDtypeStruct((rows, cols), F32), jax.ShapeDtypeStruct(shape, F32)],
        scratch_shapes=QuadScatter.scratch(rows, cols, parts) + RingScatter.scratch(n, spec[0], spec[2]),
        compiler_params=comm_params(collective_id),
    )(partial, grad)


def gather_scatter_kernel(n, spec, start, rows, parts, mine, grad, out, total, *scratch):
    count = len(QuadGather.scratch(parts))
    quad = QuadGather(rows, parts, mine, out, scratch[:count])
    ring = RingScatter(n, *spec, (rows_of(grad, spec[1][0], start, spec[0][0][0]),), (total,), scratch[count:])
    meet(quad, ring)
    quad.start()
    ring.start()
    interleave(ring, quad, n)
    quad.finish()
    ring.finish()


def gather_and_scatter(mine, grad, shape, kind, start, n, collective_id, parts=4):
    rows, cols = mine.shape
    spec = ([shape], (kind,), (2,))
    return pl.pallas_call(
        functools.partial(gather_scatter_kernel, n, spec, start, rows, parts),
        in_specs=[ANYWHERE, ANYWHERE],
        out_specs=[ANYWHERE, IN_VMEM],
        out_shape=[jax.ShapeDtypeStruct((4 * rows, cols), BF), jax.ShapeDtypeStruct(shape, F32)],
        scratch_shapes=QuadGather.scratch(parts) + RingScatter.scratch(n, spec[0], spec[2]),
        compiler_params=comm_params(collective_id),
    )(mine, grad)


def row_sums(weight, grad):
    ones = jnp.ones((8, weight.shape[1]), F32)
    return lax.dot_general(
        ones, weight.astype(F32) * grad, (((1,), (1,)), ((), ())), precision=lax.Precision.HIGHEST,
        preferred_element_type=F32)


def last_kernel(
    n, spec, rows, parts, misc_at, partial, grad, small, packed, pair, pair_sum, gains,
    result, total, small_total, misc_total, *scratch,
):
    quad_n = len(QuadScatter.scratch(rows, 128, parts))
    ring_n = len(RingScatter.scratch(n, spec[0], spec[2]))
    quad = QuadScatter(rows, parts, partial, result, scratch[:quad_n])
    ring = RingScatter(n, *spec, (grad,), (total,), scratch[quad_n : quad_n + ring_n])
    rest = scratch[quad_n + ring_n :]
    wide = Spread("dp", n, small, rest[0], rest[1:3])
    deep = Spread("tensor", 4, rest[3], rest[4], rest[5:])
    barrier = pltpu.get_barrier_semaphore()
    pl.semaphore_wait(barrier, wide.greet(barrier) + deep.greet(barrier))
    quad.start()
    ring.start()
    wide.start()
    interleave(ring, quad, n)
    quad.finish()
    small_total[...] = wide.total()
    ring.finish()
    cols = misc_total.shape[1]
    misc = rest[3]
    local = packed.shape[0]
    misc[...] = jnp.zeros_like(misc)
    misc[0:2, :] = small_total[misc_at : misc_at + 2, 0:cols]
    gain = gains[0:2, :].astype(F32)
    misc[2:3, 0:local] = row_sums(packed[...], total[...])[0:1] / gain[0:1]
    misc[3:4, 0:local] = row_sums(pair[...], pair_sum[...])[0:1] / gain[1:2]
    deep.start()
    misc_total[...] = deep.total()


def scatter_last(partial, grad, shape, small, misc_at, misc_cols, packed, pair, pair_sum, gains, n, collective_id, parts=4):
    rows, cols = partial.shape[0] // 4, partial.shape[1]
    spec = ([shape], ("rows",), (2,))
    misc_shape = (8, misc_cols)
    return pl.pallas_call(
        functools.partial(last_kernel, n, spec, rows, parts, misc_at),
        in_specs=[ANYWHERE, ANYWHERE] + [IN_VMEM] * 5,
        out_specs=[IN_VMEM] * 4,
        out_shape=[
            jax.ShapeDtypeStruct((rows, cols), F32), jax.ShapeDtypeStruct(shape, F32),
            jax.ShapeDtypeStruct(small.shape, F32), jax.ShapeDtypeStruct(misc_shape, F32),
        ],
        scratch_shapes=QuadScatter.scratch(rows, cols, parts) + RingScatter.scratch(n, spec[0], spec[2])
        + Spread.scratch(n, small.shape) + [pltpu.VMEM(misc_shape, F32)] + Spread.scratch(4, misc_shape),
        compiler_params=comm_params(collective_id),
    )(partial, grad, small, packed, pair, pair_sum, gains)


def norm_back(values, rms_inv, gain, d_normed):
    scaled = d_normed * gain
    return rms_inv * scaled - values * rms_inv**3 * jnp.mean(scaled * values, -1, keepdims=True)


def weight_grad(source, d_target):
    return jnp.einsum("td,te->de", source, d_target, preferred_element_type=jnp.float32).astype(BF)


def back_product(d_target, weight):
    return jnp.einsum("te,de->td", d_target, weight, preferred_element_type=jnp.float32)


def body(
    inputs, lengths, loss_mask, teacher, attn_gain, q_weight, k_weight, v_weight, gating_weight,
    alpha_weight, beta_weight, q_conv, k_conv, v_conv, decay_log, decay_bias, out_gain, out_weight,
    ffn_gain, ffn_gate, ffn_up, ffn_down,
):
    seq_count, slot_n, width_n = inputs.shape
    n = lax.axis_size("dp")
    tokens_n = seq_count * slot_n
    share_n = slot_n // lax.axis_size("tensor")
    share_start = lax.axis_index("tensor") * share_n
    share_rows = seq_count * share_n
    heads = decay_log.shape[0]
    hk = q_conv.shape[1]
    hv = v_conv.shape[1]
    dk, dv = hk // heads, hv // heads
    wide = 2 * hk + hv
    unit_n = ffn_gate.shape[1]
    local_d = q_weight.shape[0]
    side = "cols" if local_d % 128 == 0 else "stack"

    def joined(whole):
        if side == "cols":
            return whole
        return whole.transpose(1, 0, 2).reshape(whole.shape[1], -1)

    def parted(grad):
        if side == "cols":
            return grad
        return grad.reshape(grad.shape[0], n, local_d).transpose(1, 0, 2)

    positions = lax.broadcasted_iota(jnp.int32, (seq_count, slot_n), 1)
    valid = (positions < lengths[:, None]).astype(jnp.float32)
    tok_weight = valid * loss_mask.astype(jnp.float32)

    packed = jnp.concatenate(
        [q_weight, k_weight, v_weight, gating_weight, alpha_weight, beta_weight,
         jnp.zeros((local_d, BLOCK - 2 * heads), BF)], 1)
    pair = jnp.concatenate([ffn_gate, ffn_up], 1)
    gains = jnp.concatenate([attn_gain[None], ffn_gain[None], jnp.zeros((30, local_d), BF)], 0)
    proj_w, gains_w, counted = gather_first(packed, gains, jnp.full((8, 128), jnp.sum(tok_weight)), n)
    count_all = counted[0, 0]
    gains_w = gains_w.reshape(n, 32, local_d)[:, :2].transpose(1, 0, 2).reshape(2, width_n).astype(jnp.float32)
    gain_attn, gain_ffn = gains_w[0], gains_w[1]

    flat_in = inputs.reshape(tokens_n, width_n).astype(jnp.float32)
    attn_rms = lax.rsqrt(jnp.mean(flat_in * flat_in, -1, keepdims=True) + 1e-06)
    normed = (flat_in * attn_rms * gain_attn).astype(BF)
    proj = jnp.dot(normed, proj_w, preferred_element_type=jnp.float32)
    taps = jnp.pad(jnp.concatenate([q_conv, k_conv, v_conv], 1), ((0, 4), (0, 0)))
    hp = jnp.concatenate([-jnp.exp(decay_log)[None], decay_bias[None], jnp.zeros((6, heads), F32)], 0)
    hp = jnp.pad(hp, ((0, 0), (0, BLOCK - heads)))
    mixed_low, mix_out, fresh, inverse, states, out_w, pair_w = delta_forward(
        proj, taps, hp, out_gain[None], (out_weight, pair), (side, "rows"), n, heads, dk, dv)
    out_w = joined(out_w)
    attn_part = jnp.dot(mixed_low, out_w, preferred_element_type=jnp.float32).astype(BF)

    def share_of(array):
        return lax.dynamic_slice_in_dim(array, share_start, share_n, 1)

    early = unit_n * 6 // 11
    late = unit_n - early
    attn_own, down_w = scatter_and_gather(attn_part, ffn_down, side, 0, early, n, 3)
    base_in = share_of(inputs).reshape(share_rows, width_n).astype(jnp.float32)
    base_rms = lax.rsqrt(jnp.mean(base_in * base_in, -1, keepdims=True) + 1e-06)
    row_weight = share_of(tok_weight).reshape(share_rows, 1)
    row_valid = share_of(valid).reshape(share_rows, 1)
    row_teacher = share_of(teacher).reshape(share_rows, width_n).astype(jnp.float32)
    resid = base_in + attn_own
    ffn_rms = lax.rsqrt(jnp.mean(resid * resid, -1, keepdims=True) + 1e-06)
    normed_own = (resid * ffn_rms * gain_ffn).astype(BF)
    normed_ffn, down_w = gather_and_gather(normed_own, ffn_down, down_w, side, early, late, n, 4)
    down_w = joined(down_w)
    pre = jnp.dot(normed_ffn, pair_w, preferred_element_type=jnp.float32)
    gate_pre, up_pre = pre[:, :unit_n], pre[:, unit_n:]
    sig_gate = jax.nn.sigmoid(gate_pre)
    silu_gate = gate_pre * sig_gate
    hidden = (silu_gate * up_pre).astype(BF)
    ffn_part = jnp.dot(hidden, down_w, preferred_element_type=jnp.float32).astype(BF)
    output = resid + scatter_rows(ffn_part, 5)
    error = (output - row_teacher) * row_weight
    coef = 0.5 * tokens_n * n / count_all
    d_output = 2.0 * coef * error * row_weight
    d_ffn = gather_rows(d_output.astype(BF), 6)
    down_grad = parted(weight_grad(hidden, d_ffn))
    d_hidden = back_product(d_ffn, down_w)
    d_gate = (d_hidden * up_pre * sig_gate * (1.0 + gate_pre * (1.0 - sig_gate))).astype(BF)
    d_up = (d_hidden * silu_gate).astype(BF)
    d_pair = jnp.concatenate([d_gate, d_up], 1)
    pair_grad = weight_grad(normed_ffn, d_pair)
    d_nffn, down_early = scatter_and_scatter(
        back_product(d_pair, pair_w).astype(BF), down_grad, (early, local_d), side, 0, n, 7)
    d_resid = d_output + norm_back(resid, ffn_rms, gain_ffn, d_nffn)
    d_attn, down_late = gather_and_scatter(d_resid.astype(BF), down_grad, (late, local_d), side, early, n, 8)
    out_grad = parted(weight_grad(mixed_low, d_attn))
    d_mixed = back_product(d_attn, out_w).astype(BF)
    d_proj, tap_grad, hp_grad, out_gain_part, out_sum, pair_sum = delta_backward(
        proj, taps, hp, out_gain[None], mix_out, fresh, inverse, states, d_mixed,
        (out_grad, pair_grad), (out_weight.shape, pair.shape), (side, "rows"), n, heads, dk, dv)
    proj_grad = weight_grad(normed, d_proj)
    d_norm_part = back_product(d_proj, proj_w).astype(BF)

    def line(values):
        return jnp.pad(values, ((0, 0), (0, wide - values.shape[1])))

    small = jnp.concatenate(
        [tap_grad[:4], line(hp_grad[:2]), line(out_gain_part), jnp.full((1, wide), jnp.sum(error * error))], 0)
    misc_cols = max(dv, -(-local_d // 128) * 128)
    d_norm, proj_sum, small_sum, misc_sum = scatter_last(
        d_norm_part, proj_grad, packed.shape, small, 6, misc_cols, packed, pair, pair_sum, gains, n, 10)
    input_grad = (d_resid + norm_back(base_in, base_rms, gain_attn, d_norm)).reshape(seq_count, share_n, width_n)
    activations = (output * row_valid).astype(BF).reshape(seq_count, share_n, width_n)
    loss = misc_sum[1, 0] / count_all
    return (
        activations, loss, input_grad, misc_sum[2, :local_d],
        proj_sum[:, :hk], proj_sum[:, hk : 2 * hk], proj_sum[:, 2 * hk : wide], proj_sum[:, wide : wide + hv],
        proj_sum[:, wide + hv : wide + hv + heads], proj_sum[:, wide + hv + heads : wide + hv + 2 * heads],
        small_sum[:4, :hk], small_sum[:4, hk : 2 * hk], small_sum[:4, 2 * hk : wide],
        small_sum[4, :heads], small_sum[5, :heads], misc_sum[0, :dv],
        out_sum, misc_sum[3, :local_d], pair_sum[:, :unit_n], pair_sum[:, unit_n:],
        jnp.concatenate([down_early, down_late], 0),
    )


def solution(mesh):
    both = P("dp", "tensor")
    rows = P("dp", "tensor", None)
    flip = P("tensor", "dp")
    taps = P(None, "tensor")
    return jax.shard_map(
        body,
        mesh=mesh,
        in_specs=(
            P("dp", None, None), P("dp"), P("dp", None), P("dp", None, None), P("dp"),
            both, both, both, both, both, both, taps, taps, taps,
            P("tensor"), P("tensor"), P(), flip, P("dp"), both, both, flip,
        ),
        out_specs=(
            rows, P(), rows, P("dp"), both, both, both, both, both, both,
            taps, taps, taps, P("tensor"), P("tensor"), P(), flip, P("dp"), both, both, flip,
        ),
        check_vma=False,
    )
```
